32 devices in a mesh: grp: 2 (over x), seq: 4 (over y, core), head: 4 (over z).
Axes of the slice: x: 2, y: 2, z: 4, core: 2. Of those that a mesh axis runs over, the one named last changes fastest.
Arguments:
- queries: bfloat16 [4096, 4096], P(('grp', 'seq'), 'head'), parts along dimension 0, may hold values from -200 to 200
- keys: bfloat16 [4096, 1024], P(('grp', 'seq'), 'head'), parts along dimension 0, may hold values from -7 to 7
- values: bfloat16 [4096, 1024], P(('grp', 'seq'), 'head'), parts along dimension 0, may hold values from -18 to 18
- doc_ids: int32 [4096], P(('grp', 'seq')), parts along dimension 0, may hold values from 0 to 2, never falling along the last dimension, each value on 1 to 1024 neighbouring positions
- output_cotangent: bfloat16 [4096, 4096], P(('grp', 'seq'), 'head'), parts along dimension 0, may hold values from -6 to 6
Outputs:
- attended: bfloat16 [4096, 4096], P(('grp', 'seq'), 'head'), parts along dimension 0
- grad_queries: bfloat16 [4096, 4096], P(('grp', 'seq'), 'head'), parts along dimension 0
- grad_keys: bfloat16 [4096, 1024], P(('grp', 'seq'), 'head'), parts along dimension 0
- grad_values: bfloat16 [4096, 1024], P(('grp', 'seq'), 'head'), parts along dimension 0
The draws below stay inside these ranges and needn't reach their ends.
There are 2 independent parts, one for each index of `grp`. The reference program is written for one: setup_inputs(seed, part) draws one part's arguments, and reference() takes and returns one part's arrays. A program takes and returns all parts, laid end to end along the dimension named above; each array names one. Nothing has to cross between parts.
All inputs are finite; a program needn't handle non-finite values.
Results may differ from the reference program's by a relative error of at most 0.02.
Values may be sent and summed in bfloat16 or wider, within the bound.
No kernel may reach another device: no remote copies, remote signals or barrier semaphores. Data moves between devices by JAX's collectives and lax.ppermute only.
A program may use at most 128 MiB of HBM per device.

```python
import math
import jax
import jax.numpy as jnp
import numpy as np
from jax import lax

QUERY_HEADS = 32
KEY_VALUE_HEADS = 8
HEAD_SIZE = 128
WINDOW = 2048
TOKENS_PER_SHARD = 512
DOCS = 3
QUERY_PER_KV = 4
PACKED_TOKENS = 2048
DOC_MOST = 1024
N_SEQ = 4


def key_base(key):
    return jnp.clip(jax.random.normal(jax.random.fold_in(key, 7), (PACKED_TOKENS, KEY_VALUE_HEADS * HEAD_SIZE), jnp.float32), -6.0, 6.0)


def draw_keys(key, part):
    offset_start = key_base(key)
    return offset_start.astype(jnp.bfloat16)


def draw_queries(key, part):
    drawn = jnp.clip(jax.random.normal(jax.random.fold_in(key, 11), (PACKED_TOKENS, QUERY_HEADS * HEAD_SIZE), jnp.float32), -6.0, 6.0) * 2.0
    return drawn.astype(jnp.bfloat16)


def levels(own_key, shape, split, low, largest):
    def one(position, parts):
        draws = jax.random.uniform(jax.random.fold_in(jax.random.fold_in(own_key, 6), position), (parts,), jnp.float32, low / len(split), largest / len(split))
        return jnp.repeat(jnp.exp(draws), shape[position] // parts).reshape((-1,) + (1,) * (len(shape) - position - 1))

    gain = one(*split[0])
    for cut in split[1:]:
        gain = gain * one(*cut)
    return gain


def length_profile(count, total, bound, slope):
    weights = [(1 << 20) // math.isqrt(rank ** slope) + 1 for rank in range(2, count + 1)]
    spare, holding = total - bound - (count - 1), [1] * (count - 1)
    while spare > 0:
        movable = [i for i in range(count - 1) if holding[i] < bound]
        mass, remaining = sum([weights[i] for i in movable]), spare
        for i in movable:
            more = min(bound - holding[i], max(1, remaining * weights[i] // mass), spare)
            holding[i] = holding[i] + more
            spare = spare - more
    return np.array([bound] + holding)


def ragged(rng, count, total, most, slope):
    if count == 2:
        one = jax.random.randint(rng, (), max(1, total - most), min(most, total - 1) + 1)
        return jnp.stack([one, total - one])
    tallies = jnp.asarray(length_profile(count, total, most, slope), jnp.int32)
    twos = (count - 1) // 2
    giver, sink = tallies[1:1 + 2 * twos:2], tallies[2:2 + 2 * twos:2]
    room = jnp.minimum(giver - 1, most - sink)
    passed = jax.random.randint(jax.random.fold_in(rng, 1), (twos,), 0, 1 << 20) % (room + 1)
    tallies = tallies.at[1:1 + 2 * twos:2].set(giver - passed).at[2:2 + 2 * twos:2].set(sink + passed)
    return tallies[jax.random.permutation(jax.random.fold_in(rng, 2), count)]


def normal_values(own_key, shape, scale, most, shards=(), held_as=jnp.bfloat16):
    result = scale * jax.random.normal(own_key, shape, jnp.float32)
    if shards:
        result = result * levels(own_key, shape, shards, -0.22, 0.18)
    return jnp.clip(result, -most, most).astype(held_as)


def setup_inputs(seed: int = 0, part: int = 0) -> dict:
    arg_keys = jax.random.split(jax.random.key(seed), 6)
    part_splits = jax.random.split(jax.random.fold_in(arg_keys[5], part), 6)
    return {
        "queries": draw_queries(jax.random.fold_in(jax.random.fold_in(arg_keys[5], part), 71), part),
        "keys": draw_keys(jax.random.fold_in(jax.random.fold_in(arg_keys[5], part), 71), part),
        "values": normal_values(part_splits[2], (PACKED_TOKENS, KEY_VALUE_HEADS * HEAD_SIZE), 3.0, 18.0, ((0, 4), (1, 4))),
        "doc_ids": jnp.searchsorted(jnp.cumsum(ragged(part_splits[3], DOCS, PACKED_TOKENS, DOC_MOST, 1)), jnp.arange(PACKED_TOKENS), side="right").astype(jnp.int32),
        "output_cotangent": normal_values(part_splits[4], (PACKED_TOKENS, QUERY_HEADS * HEAD_SIZE), 1.0, 6.0, ((0, 4), (1, 4))),
    }


NEG_FILL = -1.0e30


def reference(queries, keys, values, doc_ids, output_cotangent):
    scale = HEAD_SIZE ** -0.5
    block_width = KEY_VALUE_HEADS * HEAD_SIZE
    window_extent = WINDOW + TOKENS_PER_SHARD
    padded_keys = jnp.concatenate([jnp.zeros((WINDOW, block_width), jnp.bfloat16), keys], 0)
    padded_values = jnp.concatenate([jnp.zeros((WINDOW, block_width), jnp.bfloat16), values], 0)
    docs_pad = jnp.concatenate([jnp.full((WINDOW,), -1, jnp.int32), doc_ids], 0)
    offsets = jnp.arange(TOKENS_PER_SHARD, dtype=jnp.int32)
    key_offsets = jnp.arange(window_extent, dtype=jnp.int32)

    def step(carry, index):
        grad_k, grad_v = carry
        first_position = (index * TOKENS_PER_SHARD).astype(jnp.int32)
        query_block = lax.dynamic_slice_in_dim(queries, first_position, TOKENS_PER_SHARD, 0).astype(jnp.float32).reshape(TOKENS_PER_SHARD, KEY_VALUE_HEADS, QUERY_PER_KV, HEAD_SIZE)
        grad_output_block = lax.dynamic_slice_in_dim(output_cotangent, first_position, TOKENS_PER_SHARD, 0).astype(jnp.float32).reshape(TOKENS_PER_SHARD, KEY_VALUE_HEADS, QUERY_PER_KV, HEAD_SIZE)
        doc_q = lax.dynamic_slice_in_dim(doc_ids, first_position, TOKENS_PER_SHARD, 0)
        key_block = lax.dynamic_slice_in_dim(padded_keys, first_position, window_extent, 0).astype(jnp.float32).reshape(window_extent, KEY_VALUE_HEADS, HEAD_SIZE)
        value_block = lax.dynamic_slice_in_dim(padded_values, first_position, window_extent, 0).astype(jnp.float32).reshape(window_extent, KEY_VALUE_HEADS, HEAD_SIZE)
        doc_k = lax.dynamic_slice_in_dim(docs_pad, first_position, window_extent, 0)
        q_pos = first_position + offsets
        k_pos = first_position - WINDOW + key_offsets
        diff = q_pos[:, None] - k_pos[None, :]
        live = (doc_q[:, None] == doc_k[None, :]) & (diff >= 0) & (diff < WINDOW) & (k_pos[None, :] >= 0)
        scores = jnp.einsum('ighd,jgd->ghij', query_block, key_block) * scale
        masked = jnp.where(live, scores, NEG_FILL)
        top = jnp.max(masked, axis=-1, keepdims=True)
        expo = jnp.where(live, jnp.exp(masked - top), 0.0)
        total = jnp.sum(expo, axis=-1, keepdims=True)
        prob = expo / total
        weights = lax.optimization_barrier(prob.astype(jnp.bfloat16)).astype(jnp.float32)
        out_f = jnp.einsum('ghij,jgd->ighd', weights, value_block)
        out_b = out_f.astype(jnp.bfloat16)
        out_back = lax.optimization_barrier(out_b).astype(jnp.float32)
        delta = jnp.transpose(jnp.sum(grad_output_block * out_back, axis=-1), (1, 2, 0))
        dprob = jnp.einsum('ighd,jgd->ghij', grad_output_block, value_block)
        dscore = lax.optimization_barrier((prob * (dprob - delta[..., None])).astype(jnp.bfloat16)).astype(jnp.float32)
        dq_blk = (scale * jnp.einsum('ghij,jgd->ighd', dscore, key_block)).astype(jnp.bfloat16)
        dk_blk = scale * jnp.einsum('ghij,ighd->jgd', dscore, query_block)
        dv_blk = jnp.einsum('ghij,ighd->jgd', weights, grad_output_block)
        grad_k = lax.dynamic_update_slice_in_dim(grad_k, lax.dynamic_slice_in_dim(grad_k, first_position, window_extent, 0) + dk_blk.reshape(window_extent, block_width), first_position, 0)
        grad_v = lax.dynamic_update_slice_in_dim(grad_v, lax.dynamic_slice_in_dim(grad_v, first_position, window_extent, 0) + dv_blk.reshape(window_extent, block_width), first_position, 0)
        return (grad_k, grad_v), (out_b.reshape(TOKENS_PER_SHARD, QUERY_HEADS * HEAD_SIZE), dq_blk.reshape(TOKENS_PER_SHARD, QUERY_HEADS * HEAD_SIZE))

    init = (jnp.zeros((WINDOW + PACKED_TOKENS, block_width), jnp.float32), jnp.zeros((WINDOW + PACKED_TOKENS, block_width), jnp.float32))
    (grad_k, grad_v), (outs, dqs) = lax.scan(step, init, jnp.arange(N_SEQ, dtype=jnp.int32))
    attended = outs.reshape(PACKED_TOKENS, QUERY_HEADS * HEAD_SIZE)
    grad_queries = dqs.reshape(PACKED_TOKENS, QUERY_HEADS * HEAD_SIZE)
    return attended, grad_queries, grad_k[WINDOW:].astype(jnp.bfloat16), grad_v[WINDOW:].astype(jnp.bfloat16)
```

```python
import functools
import math

import jax
import jax.numpy as jnp
from jax import lax
from jax.experimental import pallas as pl
from jax.experimental.pallas import tpu as pltpu
from jax.sharding import PartitionSpec as P

HEAD_SIZE = 128
WINDOW = 2048
DOCS = 3

NEG_FILL = -1e30
F32 = jnp.float32
BF16 = jnp.bfloat16
SCALE = 1.0 / math.sqrt(HEAD_SIZE)
LOG2_SCALE = math.log2(math.e) / math.sqrt(HEAD_SIZE)


def from_behind(value, axis, steps):
    count = lax.axis_size(axis)
    first, last = (max(0, -steps), min(count, count - steps))
    return lax.ppermute(value, axis, [(source, source + steps) for source in range(first, last)])


def dot(a, b):
    return lax.dot_general(a, b, (((1,), (0,)), ((), ())), preferred_element_type=F32)


def fold_rows(value, op):
    total = value[0:8]
    for j in range(8, value.shape[0], 8):
        total = op(total, value[j : j + 8])
    return total


def attend_body(tok, reach, group, tq, tk, scal, q_ref, do_ref, *rest):
    nb = reach + 1
    k_refs, v_refs = rest[:nb], rest[nb : 2 * nb]
    o_ref, dq_ref = rest[2 * nb : 2 * nb + 2]
    far_refs = rest[2 * nb + 2 : 3 * nb + 1]
    dk_ref, dv_ref = rest[3 * nb + 1 : 3 * nb + 3]
    k_all, v_all, kt_all, vt_all, dk_all, dv_all, s_buf, e_buf, acc, top, total = rest[3 * nb + 3 :]
    tile, tiles = pl.program_id(1), pl.num_programs(1)
    start_1, start_2, q_first = scal[0], scal[1], scal[2]

    @pl.when(tile == 0)
    def _():
        for b in range(nb):
            k_all[b * tok : (b + 1) * tok, :] = k_refs[b][...]
            v_all[b * tok : (b + 1) * tok, :] = v_refs[b][...]
            kt_all[:, b * tok : (b + 1) * tok] = k_refs[b][...].T
            vt_all[:, b * tok : (b + 1) * tok] = v_refs[b][...].T
        dk_all[...] = jnp.zeros_like(dk_all)
        dv_all[...] = jnp.zeros_like(dv_all)

    k_base = q_first - reach * tok
    q_pos = q_first + tile * tq

    def first_live(i):
        doc_start = jnp.where(i < start_1, 0, jnp.where(i < start_2, start_1, start_2))
        return jnp.maximum(doc_start, i - (WINDOW - 1))

    low = jnp.maximum(first_live(q_pos) - k_base, 0) // tk
    high = (q_pos + tq - 1 - k_base) // tk + 1
    last_first = first_live(q_pos + tq - 1)
    heads = range(group)
    q = jnp.concatenate([q_ref[:, h * HEAD_SIZE : (h + 1) * HEAD_SIZE] for h in heads], 0)
    qt = jnp.concatenate([q_ref[:, h * HEAD_SIZE : (h + 1) * HEAD_SIZE].T for h in heads], 1)
    top[...] = jnp.full_like(top, NEG_FILL)

    def scores(t, carry):
        off = pl.multiple_of(t * tk, tk)
        s = dot(k_all[pl.ds(off, tk), :], qt)
        k_pos = k_base + off
        full = (k_pos >= last_first) & (k_pos + tk - 1 <= q_pos)

        def put(s):
            s_buf[pl.ds(off, tk), :] = s
            top[...] = jnp.maximum(top[...], fold_rows(s, jnp.maximum))

        @pl.when(full)
        def _():
            put(s)

        @pl.when(jnp.logical_not(full))
        def _():
            j = k_pos + lax.broadcasted_iota(jnp.int32, (tk, tq), 0)
            i = q_pos + lax.broadcasted_iota(jnp.int32, (tk, tq), 1)
            first = first_live(q_pos + lax.broadcasted_iota(jnp.int32, (1, tq), 1))
            live = (j <= i) & (j >= first)
            put(jnp.concatenate([jnp.where(live, s[:, h * tq : (h + 1) * tq], NEG_FILL) for h in heads], 1))

        return carry

    lax.fori_loop(low, high, scores, 0)
    m = jnp.max(top[...], axis=0, keepdims=True)
    total[...] = jnp.zeros_like(total)
    acc[...] = jnp.zeros_like(acc)

    def weigh(t, carry):
        off = pl.multiple_of(t * tk, tk)
        e = jnp.exp2((s_buf[pl.ds(off, tk), :] - m) * LOG2_SCALE)
        total[...] += fold_rows(e, jnp.add)
        eb = e.astype(BF16)
        e_buf[pl.ds(off, tk), :] = eb
        acc[...] += dot(vt_all[:, pl.ds(off, tk)], eb)
        return carry

    lax.fori_loop(low, high, weigh, 0)
    inverse = 1.0 / jnp.sum(total[...], axis=0, keepdims=True)
    out_t = (acc[...] * inverse).astype(BF16)
    for h in heads:
        o_ref[:, h * HEAD_SIZE : (h + 1) * HEAD_SIZE] = out_t[:, h * tq : (h + 1) * tq].T
    do_t = jnp.concatenate([do_ref[:, h * HEAD_SIZE : (h + 1) * HEAD_SIZE].T for h in heads], 1)
    do_t = (do_t.astype(F32) * inverse).astype(BF16)
    delta = jnp.sum(do_t.astype(F32) * out_t.astype(F32), axis=0, keepdims=True)
    do = jnp.concatenate([do_t[:, h * tq : (h + 1) * tq].T for h in heads], 0)
    acc[...] = jnp.zeros_like(acc)

    def back(t, carry):
        off = pl.multiple_of(t * tk, tk)
        eb = e_buf[pl.ds(off, tk), :]
        dp = dot(v_all[pl.ds(off, tk), :], do_t)
        ds = (eb.astype(F32) * (dp - delta)).astype(BF16)
        acc[...] += dot(kt_all[:, pl.ds(off, tk)], ds)
        dk_all[pl.ds(off, tk), :] += dot(ds, q)
        dv_all[pl.ds(off, tk), :] += dot(eb, do)
        return carry

    lax.fori_loop(low, high, back, 0)
    dq_t = (acc[...] * SCALE).astype(BF16)
    for h in heads:
        dq_ref[:, h * HEAD_SIZE : (h + 1) * HEAD_SIZE] = dq_t[:, h * tq : (h + 1) * tq].T

    @pl.when(tile == tiles - 1)
    def _():
        for b in range(reach):
            rows = slice(b * tok, (b + 1) * tok)
            far_refs[b][:, :HEAD_SIZE] = (dk_all[rows, :] * SCALE).astype(BF16)
            far_refs[b][:, HEAD_SIZE:] = dv_all[rows, :].astype(BF16)
        dk_ref[...] = dk_all[reach * tok :, :] * SCALE
        dv_ref[...] = dv_all[reach * tok :, :]


def attend(scal, q, do, key_blocks, value_blocks):
    tok = q.shape[0]
    kv_heads = key_blocks[-1][0].shape[1] // HEAD_SIZE
    group = q.shape[1] // HEAD_SIZE // kv_heads
    reach = len(key_blocks) - 1
    tq = tk = min(256, tok)
    wide = group * tq
    q_spec = pl.BlockSpec((tq, group * HEAD_SIZE), lambda g, i, s: (i, g))

    def kv_spec(first):
        return pl.BlockSpec((tok, HEAD_SIZE), lambda g, i, s, first=first: (0, g + first))

    far_spec = pl.BlockSpec((tok, 2 * HEAD_SIZE), lambda g, i, s: (0, g))
    keys_seen = (reach + 1) * tok
    results = pl.pallas_call(
        functools.partial(attend_body, tok, reach, group, tq, tk),
        grid_spec=pltpu.PrefetchScalarGridSpec(
            num_scalar_prefetch=1,
            grid=(kv_heads, tok // tq),
            in_specs=[q_spec, q_spec] + [kv_spec(f) for _, f in key_blocks] + [kv_spec(f) for _, f in value_blocks],
            out_specs=[q_spec, q_spec] + [far_spec] * reach + [kv_spec(0)] * 2,
            scratch_shapes=[
                pltpu.VMEM((keys_seen, HEAD_SIZE), BF16),
                pltpu.VMEM((keys_seen, HEAD_SIZE), BF16),
                pltpu.VMEM((HEAD_SIZE, keys_seen), BF16),
                pltpu.VMEM((HEAD_SIZE, keys_seen), BF16),
                pltpu.VMEM((keys_seen, HEAD_SIZE), F32),
                pltpu.VMEM((keys_seen, HEAD_SIZE), F32),
                pltpu.VMEM((keys_seen, wide), F32),
                pltpu.VMEM((keys_seen, wide), BF16),
                pltpu.VMEM((HEAD_SIZE, wide), F32),
                pltpu.VMEM((8, wide), F32),
                pltpu.VMEM((8, wide), F32),
            ],
        ),
        out_shape=[jax.ShapeDtypeStruct(q.shape, BF16)] * 2
        + [jax.ShapeDtypeStruct((tok, 2 * kv_heads * HEAD_SIZE), BF16)] * reach
        + [jax.ShapeDtypeStruct((tok, kv_heads * HEAD_SIZE), F32)] * 2,
        compiler_params=pltpu.CompilerParams(vmem_limit_bytes=56 << 20),
        cost_estimate=pl.CostEstimate(flops=20 * 10**9, bytes_accessed=8 << 20, transcendentals=8 * tok * tok),
        name="attend",
    )(scal, q, do, *[a for a, _ in key_blocks], *[a for a, _ in value_blocks])
    return results[0], results[1], results[2 : 2 + reach], results[2 + reach], results[3 + reach]


def on_device(queries, keys, values, doc_ids, output_cotangent):
    tok, kv_width = keys.shape
    kv_heads = kv_width // HEAD_SIZE
    count = lax.axis_size("seq")
    rank = lax.axis_index("seq")
    span = min(WINDOW, tok * count // 2)
    reach = min((span + tok - 2) // tok, count - 1)
    packed = jnp.concatenate([keys, values], 1)
    far = [from_behind(packed, "seq", dist) for dist in range(1, reach + 1)]
    before = jnp.stack([jnp.sum((doc_ids < d).astype(jnp.int32)) for d in range(1, DOCS)])
    starts = lax.psum(before, "seq")
    scal = jnp.concatenate([starts, (rank * tok)[None].astype(jnp.int32)])
    key_blocks = [(block, 0) for block in far[::-1]] + [(keys, 0)]
    value_blocks = [(block, kv_heads) for block in far[::-1]] + [(values, 0)]
    attended, grad_queries, parts, grad_k, grad_v = attend(
        scal, queries, output_cotangent, key_blocks, value_blocks
    )
    for dist in range(1, reach + 1):
        back = from_behind(parts[reach - dist], "seq", -dist).reshape(tok, kv_heads, 2, HEAD_SIZE)
        grad_k = grad_k + back[:, :, 0].reshape(tok, kv_width).astype(F32)
        grad_v = grad_v + back[:, :, 1].reshape(tok, kv_width).astype(F32)
    return attended, grad_queries, grad_k.astype(BF16), grad_v.astype(BF16)


def solution(mesh):
    wide = P(("grp", "seq"), "head")
    in_specs = (wide, wide, wide, P(("grp", "seq")), wide)
    return jax.shard_map(
        on_device, mesh=mesh, in_specs=in_specs, out_specs=(wide,) * 4, check_vma=False
    )
```

```python
import functools
import math

import jax
import jax.numpy as jnp
from jax import lax
from jax.experimental import pallas as pl
from jax.experimental.pallas import tpu as pltpu
from jax.sharding import PartitionSpec as P

HEAD_SIZE = 128
WINDOW = 2048
DOCS = 3

NEG_FILL = -1e30
F32 = jnp.float32
BF16 = jnp.bfloat16
SCALE = 1.0 / math.sqrt(HEAD_SIZE)
LOG2_SCALE = math.log2(math.e) / math.sqrt(HEAD_SIZE)
VMEM_LIMIT = 56 << 20


def from_behind(value, steps):
    count = lax.axis_size("seq")
    first, last = (max(0, -steps), min(count, count - steps))
    return lax.ppermute(value, "seq", [(source, source + steps) for source in range(first, last)])


def dot(a, b, ca=1, cb=0):
    return lax.dot_general(a, b, (((ca,), (cb,)), ((), ())), preferred_element_type=F32)


def fold_rows(value, op):
    total = value[0:8]
    for j in range(8, value.shape[0], 8):
        total = op(total, value[j : j + 8])
    return total


def attend_body(tok, reach, group, tq, tk, loads, stores, starts, q_ref, do_ref, own_k, own_v, *rest):
    far_in, rest = rest[: 2 * len(loads)], rest[2 * len(loads) :]
    o_ref, dq_ref, dk_ref, dv_ref = rest[:4]
    far_out, rest = rest[4 : 4 + len(stores)], rest[4 + len(stores) :]
    k_all, v_all, kt_all, vt_all, dk_all, dv_all, s_buf, e_buf, acc, top, total = rest
    tile, tiles = pl.program_id(1), pl.num_programs(1)
    rank = lax.axis_index("seq")
    start_1, start_2, q_first = starts[0], starts[1], rank * tok
    k_base = q_first - reach * tok
    q_pos = q_first + tile * tq
    heads = range(group)

    def first_live(i):
        doc_start = jnp.where(i < start_1, 0, jnp.where(i < start_2, start_1, start_2))
        return jnp.maximum(doc_start, i - (WINDOW - 1))

    def load(first, k_ref, v_ref):
        k, v = k_ref[...], v_ref[...]
        rows = slice(first, first + k.shape[0])
        k_all[rows, :], v_all[rows, :] = k, v
        kt_all[:, rows], vt_all[:, rows] = k.T, v.T
        dk_all[rows, :] = jnp.zeros(k.shape, F32)
        dv_all[rows, :] = jnp.zeros(v.shape, F32)

    @pl.when(tile == 0)
    def _():
        needed = first_live(q_first) - k_base
        load(reach * tok, own_k, own_v)
        for n, (first, when) in enumerate(loads):
            k_ref, v_ref = far_in[2 * n : 2 * n + 2]
            pl.when(when(rank) & (needed < first + k_ref.shape[0]))(functools.partial(load, first, k_ref, v_ref))

    low = jnp.maximum(first_live(q_pos) - k_base, 0) // tk
    high = (q_pos + tq - 1 - k_base) // tk + 1
    last_first = first_live(q_pos + tq - 1)

    def over_keys(visit):
        def two(n, carry):
            visit(pl.multiple_of((low + 2 * n) * tk, tk), 2 * tk)
            return carry

        lax.fori_loop(0, (high - low) // 2, two, 0)

        @pl.when((high - low) % 2 == 1)
        def _():
            visit(pl.multiple_of((high - 1) * tk, tk), tk)

    q = jnp.concatenate([q_ref[:, h * HEAD_SIZE : (h + 1) * HEAD_SIZE] for h in heads], 0)
    do = jnp.concatenate([do_ref[:, h * HEAD_SIZE : (h + 1) * HEAD_SIZE] for h in heads], 0)
    top[...] = jnp.full_like(top, NEG_FILL)

    def scores(off, size):
        s = dot(k_all[pl.ds(off, size), :], q, 1, 1)
        k_pos = k_base + off
        full = (k_pos >= last_first) & (k_pos + size - 1 <= q_pos)

        def put(s):
            s_buf[pl.ds(off, size), :] = s
            top[...] = jnp.maximum(top[...], fold_rows(s, jnp.maximum))

        @pl.when(full)
        def _():
            put(s)

        @pl.when(jnp.logical_not(full))
        def _():
            j = k_pos + lax.broadcasted_iota(jnp.int32, (size, tq), 0)
            i = q_pos + lax.broadcasted_iota(jnp.int32, (size, tq), 1)
            first = first_live(q_pos + lax.broadcasted_iota(jnp.int32, (1, tq), 1))
            live = (j <= i) & (j >= first)
            put(jnp.concatenate([jnp.where(live, s[:, h * tq : (h + 1) * tq], NEG_FILL) for h in heads], 1))

    over_keys(scores)
    m = jnp.max(top[...], axis=0, keepdims=True)
    total[...] = jnp.zeros_like(total)
    acc[...] = jnp.zeros_like(acc)

    def weigh(off, size):
        e = jnp.exp2((s_buf[pl.ds(off, size), :] - m) * LOG2_SCALE)
        total[...] += fold_rows(e, jnp.add)
        eb = e.astype(BF16)
        e_buf[pl.ds(off, size), :] = eb
        acc[...] += dot(vt_all[:, pl.ds(off, size)], eb)

    over_keys(weigh)
    inverse = 1.0 / jnp.sum(total[...], axis=0, keepdims=True)
    out_t = (acc[...] * inverse).astype(BF16)
    out = [out_t[:, h * tq : (h + 1) * tq].T for h in heads]
    for h in heads:
        o_ref[:, h * HEAD_SIZE : (h + 1) * HEAD_SIZE] = out[h]
    product = jnp.concatenate(out, 0).astype(F32) * do.astype(F32)
    product_high = product.astype(BF16)
    product_low = (product - product_high.astype(F32)).astype(BF16)
    ones = jnp.ones((8, HEAD_SIZE), BF16)
    delta = (dot(ones, product_high, 1, 1) + dot(ones, product_low, 1, 1))[0:1]
    acc[...] = jnp.zeros_like(acc)

    def back(off, size):
        p = e_buf[pl.ds(off, size), :].astype(F32) * inverse
        dp = dot(v_all[pl.ds(off, size), :], do, 1, 1)
        ds = (p * (dp - delta)).astype(BF16)
        acc[...] += dot(kt_all[:, pl.ds(off, size)], ds)
        dk_all[pl.ds(off, size), :] += dot(ds, q)
        dv_all[pl.ds(off, size), :] += dot(p.astype(BF16), do)

    over_keys(back)
    dq_t = (acc[...] * SCALE).astype(BF16)
    for h in heads:
        dq_ref[:, h * HEAD_SIZE : (h + 1) * HEAD_SIZE] = dq_t[:, h * tq : (h + 1) * tq].T

    @pl.when(tile == tiles - 1)
    def _():
        needed = first_live(q_first) - k_base
        dk_ref[...] = dk_all[reach * tok :, :] * SCALE
        dv_ref[...] = dv_all[reach * tok :, :]
        for ref, first in zip(far_out, stores):
            row = first(rank)
            rows = pl.ds(row if isinstance(row, int) else pl.multiple_of(row, 8), ref.shape[0])

            @pl.when(needed < row + ref.shape[0])
            def _(ref=ref, rows=rows):
                ref[:, :HEAD_SIZE] = (dk_all[rows, :] * SCALE).astype(BF16)
                ref[:, HEAD_SIZE:] = dv_all[rows, :].astype(BF16)

            @pl.when(needed >= row + ref.shape[0])
            def _(ref=ref):
                ref[...] = jnp.zeros_like(ref)


def attend(starts, q, do, keys, values, far, loads, stores, reach):
    tok = q.shape[0]
    kv_heads = keys.shape[1] // HEAD_SIZE
    group = q.shape[1] // HEAD_SIZE // kv_heads
    tq = tk = min(256, tok)
    wide = group * tq
    seen = (reach + 1) * tok
    q_spec = pl.BlockSpec((tq, group * HEAD_SIZE), lambda g, i, s: (i, g))

    def kv_spec(rows, first):
        return pl.BlockSpec((rows, HEAD_SIZE), lambda g, i, s, first=first: (0, g + first))

    far_args, far_specs = [], []
    for n, _, _ in loads:
        far_args += [far[n], far[n]]
        far_specs += [kv_spec(far[n].shape[0], 0), kv_spec(far[n].shape[0], kv_heads)]
    results = pl.pallas_call(
        functools.partial(
            attend_body, tok, reach, group, tq, tk, [(r, w) for _, r, w in loads], [f for _, f in stores]
        ),
        grid_spec=pltpu.PrefetchScalarGridSpec(
            num_scalar_prefetch=1,
            grid=(kv_heads, tok // tq),
            in_specs=[q_spec, q_spec, kv_spec(tok, 0), kv_spec(tok, 0)] + far_specs,
            out_specs=[q_spec, q_spec, kv_spec(tok, 0), kv_spec(tok, 0)]
            + [pl.BlockSpec((rows, 2 * HEAD_SIZE), lambda g, i, s: (0, g)) for rows, _ in stores],
            scratch_shapes=[
                pltpu.VMEM((seen, HEAD_SIZE), BF16),
                pltpu.VMEM((seen, HEAD_SIZE), BF16),
                pltpu.VMEM((HEAD_SIZE, seen), BF16),
                pltpu.VMEM((HEAD_SIZE, seen), BF16),
                pltpu.VMEM((seen, HEAD_SIZE), F32),
                pltpu.VMEM((seen, HEAD_SIZE), F32),
                pltpu.VMEM((seen, wide), F32),
                pltpu.VMEM((seen, wide), BF16),
                pltpu.VMEM((HEAD_SIZE, wide), F32),
                pltpu.VMEM((8, wide), F32),
                pltpu.VMEM((8, wide), F32),
            ],
        ),
        out_shape=[jax.ShapeDtypeStruct(q.shape, BF16)] * 2
        + [jax.ShapeDtypeStruct(keys.shape, F32)] * 2
        + [jax.ShapeDtypeStruct((rows, 2 * kv_heads * HEAD_SIZE), BF16) for rows, _ in stores],
        compiler_params=pltpu.CompilerParams(vmem_limit_bytes=VMEM_LIMIT),
        cost_estimate=pl.CostEstimate(flops=10 * 10**9, bytes_accessed=8 << 20, transcendentals=8 * tok * tok),
        name="attend",
    )(starts, q, do, keys, values, *far_args)
    return results[:4], results[4:]


def combine_body(firsts, own_k, own_v, *rest):
    parts, (k_ref, v_ref) = rest[:-2], rest[-2:]
    k, v = own_k[...], own_v[...]
    pieces = {}
    for first, part in zip(firsts, parts):
        pieces.setdefault((first, part.shape[0]), []).append(part[...].astype(F32))
    sums = {key: functools.reduce(jnp.add, found) for key, found in pieces.items()}
    for (first, rows), part in sums.items():
        if rows == k.shape[0]:
            k, v = k + part[:, :HEAD_SIZE], v + part[:, HEAD_SIZE:]
    k_ref[...], v_ref[...] = k.astype(BF16), v.astype(BF16)
    for (first, rows), part in sums.items():
        if rows != k.shape[0]:
            at = slice(first, first + rows)
            k_ref[at, :] = (k[at] + part[:, :HEAD_SIZE]).astype(BF16)
            v_ref[at, :] = (v[at] + part[:, HEAD_SIZE:]).astype(BF16)


def combine(own_k, own_v, parts):
    tok, width = own_k.shape
    spec = pl.BlockSpec((tok, HEAD_SIZE), lambda g: (0, g))
    return pl.pallas_call(
        functools.partial(combine_body, [first for first, _ in parts]),
        grid=(width // HEAD_SIZE,),
        in_specs=[spec, spec]
        + [pl.BlockSpec((part.shape[0], 2 * HEAD_SIZE), lambda g: (0, g)) for _, part in parts],
        out_specs=[spec, spec],
        out_shape=[jax.ShapeDtypeStruct(own_k.shape, BF16)] * 2,
        compiler_params=pltpu.CompilerParams(vmem_limit_bytes=VMEM_LIMIT),
        name="combine",
    )(own_k, own_v, *[part for _, part in parts])


def always(rank):
    return rank >= 0


def any_length(tok, reach, starts, queries, keys, values, output_cotangent):
    packed = jnp.concatenate([keys, values], 1)
    far = [from_behind(packed, dist) for dist in range(1, reach + 1)]
    loads = [(dist - 1, (reach - dist) * tok, always) for dist in range(1, reach + 1)]
    stores = [(tok, lambda rank, dist=dist: (reach - dist) * tok) for dist in range(1, reach + 1)]
    own, parts = attend(starts, queries, output_cotangent, keys, values, far, loads, stores, reach)
    attended, grad_queries, own_k, own_v = own
    back = [(0, from_behind(part, -dist)) for dist, part in enumerate(parts, 1)]
    return (attended, grad_queries, *combine(own_k, own_v, back))


def two_halves(tok, starts, queries, keys, values, output_cotangent):
    half = tok // 2
    ends = [(0, 1), (2, 3)]
    near = lax.ppermute(jnp.concatenate([keys, values], 1), "seq", ends)
    across_keys = 2 * tok - starts[0]
    across_queries = starts[1] - 2 * tok
    crossing = (across_keys > 0) & (across_queries > 0)
    pieces = jnp.where(crossing, (across_keys + half - 1) // half, 0)
    ends_back = [(1, 0), (3, 2)]

    def apart(near):
        own, parts = attend(
            starts, queries, output_cotangent, keys, values, [near], [(0, 0, always)], [(tok, lambda rank: 0)], 1
        )
        attended, grad_queries, own_k, own_v = own
        back = lax.ppermute(parts[0], "seq", ends_back)
        return (attended, grad_queries, *combine(own_k, own_v, [(0, back)]))

    def across(near):
        high = jnp.concatenate([keys[half:], values[half:]], 1)
        low = jnp.concatenate([keys[:half], values[:half]], 1)

        def up(number):
            def send(high, low):
                one = [lax.ppermute(x, "seq", [(1, 2)]) for x in (high, low)[:number]]
                if number <= 2:
                    on = [lax.ppermute(x, "seq", [(2, 3)]) for x in one]
                    rank = lax.axis_index("seq")
                    one = [jnp.where(rank == 3, y, x) for x, y in zip(one, on)]
                zero = [lax.ppermute(x, "seq", [(0, 2)]) for x in (high, low)[: number - 2]] if number > 2 else []
                got = one + zero
                return tuple(got + [jnp.zeros_like(high)] * (4 - len(got)))

            return send

        got = lax.switch(pieces - 1, [up(n) for n in range(1, 5)], high, low)
        on_2, on_3 = (lambda rank: rank == 2), (lambda rank: rank == 3)
        loads = [
            (0, tok, lambda rank: rank != 2),
            (1, tok + half, on_2),
            (2, tok, on_2),
            (3, half, on_2),
            (4, 0, on_2),
            (1, half, on_3),
            (2, 0, on_3),
        ]
        stores = [
            (tok, lambda rank: tok),
            (half, lambda rank: jnp.where(rank == 2, tok, 0) + half),
            (half, lambda rank: jnp.where(rank == 2, tok, 0)),
            (half, lambda rank: half),
            (half, lambda rank: 0),
        ]
        own, parts = attend(
            starts, queries, output_cotangent, keys, values, [near, *got], loads, stores, 2
        )
        attended, grad_queries, own_k, own_v = own

        def down(number):
            def send(near_part, *parts):
                back = [(0, lax.ppermute(near_part, "seq", ends_back))]
                one, zero = parts[: min(number, 2)], parts[2:number]
                if number <= 2:
                    more = [lax.ppermute(x, "seq", [(3, 2)]) for x in one]
                    one = [(x.astype(F32) + y.astype(F32)).astype(BF16) for x, y in zip(one, more)]
                for first, x in zip((half, 0), one):
                    back.append((first, lax.ppermute(x, "seq", [(2, 1)])))
                for first, x in zip((half, 0), zero):
                    back.append((first, lax.ppermute(x, "seq", [(2, 0)])))
                return combine(own_k, own_v, back)

            return send

        return (attended, grad_queries, *lax.switch(pieces - 1, [down(n) for n in range(1, 5)], *parts))

    return lax.cond(pieces > 0, across, apart, near)


def on_device(queries, keys, values, doc_ids, output_cotangent):
    tok = keys.shape[0]
    count = lax.axis_size("seq")
    numbers = lax.broadcasted_iota(jnp.int32, (DOCS - 1, 1), 0)
    before = jnp.sum((doc_ids[None, :] <= numbers).astype(jnp.int32), axis=1)
    starts = lax.psum(before, "seq")
    span = min(WINDOW, tok * count // 2)
    reach = min((span + tok - 2) // tok, count - 1)
    if count == 4 and span == 2 * tok and tok % 512 == 0:
        return tuple(two_halves(tok, starts, queries, keys, values, output_cotangent))
    return any_length(tok, reach, starts, queries, keys, values, output_cotangent)


def solution(mesh):
    wide = P(("grp", "seq"), "head")
    in_specs = (wide, wide, wide, P(("grp", "seq")), wide)
    return jax.shard_map(
        on_device, mesh=mesh, in_specs=in_specs, out_specs=(wide,) * 4, check_vma=False
    )
```

```python
import functools
import math

import jax
import jax.numpy as jnp
from jax import lax
from jax.experimental import pallas as pl
from jax.experimental.pallas import tpu as pltpu
from jax.sharding import PartitionSpec as P

HEAD_SIZE = 128
WINDOW = 2048
DOCS = 3

NEG_FILL = -1e30
F32 = jnp.float32
BF16 = jnp.bfloat16
SCALE = 1.0 / math.sqrt(HEAD_SIZE)
LOG2_SCALE = math.log2(math.e) / math.sqrt(HEAD_SIZE)
ATTEND_VMEM = 28 << 20
COMBINE_VMEM = 12 << 20


def from_behind(value, steps):
    count = lax.axis_size("seq")
    first, last = (max(0, -steps), min(count, count - steps))
    return lax.ppermute(value, "seq", [(source, source + steps) for source in range(first, last)])


def dot(a, b, ca=1, cb=0):
    return lax.dot_general(a, b, (((ca,), (cb,)), ((), ())), preferred_element_type=F32)


def fold_rows(value, op):
    total = value[0:8]
    for j in range(8, value.shape[0], 8):
        total = op(total, value[j : j + 8])
    return total


def attend_body(tok, reach, group, tq, tk, loads, stores, carried, starts, q_ref, do_ref, own_k, own_v, *rest):
    far_in, rest = rest[: 2 * len(loads)], rest[2 * len(loads) + carried :]
    o_ref, dq_ref, own_ref = rest[:3]
    far_out, rest = rest[3 : 3 + len(stores)], rest[3 + len(stores) :]
    k_all, v_all, kt_all, vt_all, dk_all, dv_all, s_buf, e_buf, acc, top, total = rest
    tile, tiles = pl.program_id(1), pl.num_programs(1)
    rank = lax.axis_index("seq")
    start_1, start_2, q_first = starts[0], starts[1], rank * tok
    k_base = q_first - reach * tok
    q_pos = q_first + tile * tq
    heads = range(group)

    def first_live(i):
        doc_start = jnp.where(i < start_1, 0, jnp.where(i < start_2, start_1, start_2))
        return jnp.maximum(doc_start, i - (WINDOW - 1))

    def load(first, k_ref, v_ref):
        k, v = k_ref[...], v_ref[...]
        rows = slice(first, first + k.shape[0])
        k_all[rows, :], v_all[rows, :] = k, v
        kt_all[:, rows], vt_all[:, rows] = k.T, v.T
        dk_all[rows, :] = jnp.zeros(k.shape, F32)
        dv_all[rows, :] = jnp.zeros(v.shape, F32)

    @pl.when(tile == 0)
    def _():
        needed = first_live(q_first) - k_base
        load(reach * tok, own_k, own_v)
        for n, (first, when) in enumerate(loads):
            k_ref, v_ref = far_in[2 * n : 2 * n + 2]
            pl.when(when(rank) & (needed < first + k_ref.shape[0]))(functools.partial(load, first, k_ref, v_ref))

    low = jnp.maximum(first_live(q_pos) - k_base, 0) // tk
    high = (q_pos + tq - 1 - k_base) // tk + 1
    last_first = first_live(q_pos + tq - 1)

    def one_by_one(visit):
        def one(n, carry):
            visit(pl.multiple_of(n * tk, tk), tk)
            return carry

        lax.fori_loop(low, high, one, 0)

    def over_keys(visit):
        def two(n, carry):
            visit(pl.multiple_of((low + 2 * n) * tk, tk), 2 * tk)
            return carry

        lax.fori_loop(0, (high - low) // 2, two, 0)

        @pl.when((high - low) % 2 == 1)
        def _():
            visit(pl.multiple_of((high - 1) * tk, tk), tk)

    q = jnp.concatenate([q_ref[:, h * HEAD_SIZE : (h + 1) * HEAD_SIZE] for h in heads], 0)
    do = jnp.concatenate([do_ref[:, h * HEAD_SIZE : (h + 1) * HEAD_SIZE] for h in heads], 0)
    top[...] = jnp.full_like(top, NEG_FILL)

    def scores(off, size):
        s = dot(k_all[pl.ds(off, size), :], q, 1, 1)
        k_pos = k_base + off
        full = (k_pos >= last_first) & (k_pos + size - 1 <= q_pos)

        def put(s):
            s_buf[pl.ds(off, size), :] = s
            top[...] = jnp.maximum(top[...], fold_rows(s, jnp.maximum))

        @pl.when(full)
        def _():
            put(s)

        @pl.when(jnp.logical_not(full))
        def _():
            j = k_pos + lax.broadcasted_iota(jnp.int32, (size, tq), 0)
            i = q_pos + lax.broadcasted_iota(jnp.int32, (size, tq), 1)
            first = first_live(q_pos + lax.broadcasted_iota(jnp.int32, (1, tq), 1))
            live = (j <= i) & (j >= first)
            put(jnp.concatenate([jnp.where(live, s[:, h * tq : (h + 1) * tq], NEG_FILL) for h in heads], 1))

    one_by_one(scores)
    m = jnp.max(top[...], axis=0, keepdims=True)
    total[...] = jnp.zeros_like(total)
    acc[...] = jnp.zeros_like(acc)

    def weigh(off, size):
        e = jnp.exp2((s_buf[pl.ds(off, size), :] - m) * LOG2_SCALE)
        total[...] += fold_rows(e, jnp.add)
        eb = e.astype(BF16)
        e_buf[pl.ds(off, size), :] = eb
        acc[...] += dot(vt_all[:, pl.ds(off, size)], eb)

    over_keys(weigh)
    inverse = 1.0 / jnp.sum(total[...], axis=0, keepdims=True)
    out_t = (acc[...] * inverse).astype(BF16)
    out = [out_t[:, h * tq : (h + 1) * tq].T for h in heads]
    for h in heads:
        o_ref[:, h * HEAD_SIZE : (h + 1) * HEAD_SIZE] = out[h]
    product = jnp.concatenate(out, 0).astype(F32) * do.astype(F32)
    product_high = product.astype(BF16)
    product_low = (product - product_high.astype(F32)).astype(BF16)
    ones = jnp.ones((8, HEAD_SIZE), BF16)
    delta = (dot(ones, product_high, 1, 1) + dot(ones, product_low, 1, 1))[0:1]
    acc[...] = jnp.zeros_like(acc)

    def back(off, size):
        p = e_buf[pl.ds(off, size), :].astype(F32) * inverse
        dp = dot(v_all[pl.ds(off, size), :], do, 1, 1)
        ds = (p * (dp - delta)).astype(BF16)
        acc[...] += dot(kt_all[:, pl.ds(off, size)], ds)
        dk_all[pl.ds(off, size), :] += dot(ds, q)
        dv_all[pl.ds(off, size), :] += dot(p.astype(BF16), do)

    over_keys(back)
    dq_t = (acc[...] * SCALE).astype(BF16)
    for h in heads:
        dq_ref[:, h * HEAD_SIZE : (h + 1) * HEAD_SIZE] = dq_t[:, h * tq : (h + 1) * tq].T

    @pl.when(tile == tiles - 1)
    def _():
        needed = first_live(q_first) - k_base
        own_ref[:, :HEAD_SIZE] = dk_all[reach * tok :, :] * SCALE
        own_ref[:, HEAD_SIZE:] = dv_all[reach * tok :, :]
        for ref, row in zip(far_out, stores):
            rows = slice(row, row + ref.shape[0])

            @pl.when(needed < row + ref.shape[0])
            def _(ref=ref, rows=rows):
                ref[:, :HEAD_SIZE] = (dk_all[rows, :] * SCALE).astype(BF16)
                ref[:, HEAD_SIZE:] = dv_all[rows, :].astype(BF16)

            @pl.when(needed >= row + ref.shape[0])
            def _(ref=ref):
                ref[...] = jnp.zeros_like(ref)


def attend(starts, q, do, keys, values, loads, stores, reach, first_head, count, carried=()):
    tok = q.shape[0]
    group = q.shape[1] // keys.shape[1]
    tq = tk = min(256, tok)
    wide = group * tq
    seen = (reach + 1) * tok
    q_spec = pl.BlockSpec((tq, group * HEAD_SIZE), lambda g, i, s: (i, g + first_head))

    def kv_spec(rows, first):
        return pl.BlockSpec((rows, HEAD_SIZE), lambda g, i, s, first=first: (0, g + first))

    far_args, far_specs = [], []
    for array, k_block, v_block, _, _ in loads:
        far_args += [array, array]
        far_specs += [kv_spec(array.shape[0], k_block), kv_spec(array.shape[0], v_block)]
    part = pl.BlockSpec((tok, 2 * HEAD_SIZE), lambda g, i, s: (0, g))
    shape = (tok, 2 * count * HEAD_SIZE)
    before = 5 + len(far_args)
    results = pl.pallas_call(
        functools.partial(
            attend_body, tok, reach, group, tq, tk, [load[3:] for load in loads], stores, len(carried)
        ),
        grid_spec=pltpu.PrefetchScalarGridSpec(
            num_scalar_prefetch=1,
            grid=(count, tok // tq),
            in_specs=[q_spec, q_spec, kv_spec(tok, first_head), kv_spec(tok, first_head)]
            + far_specs
            + [pl.BlockSpec(memory_space=pl.ANY)] * len(carried),
            out_specs=[q_spec, q_spec] + [part] * (1 + len(stores)),
            scratch_shapes=[
                pltpu.VMEM((seen, HEAD_SIZE), BF16),
                pltpu.VMEM((seen, HEAD_SIZE), BF16),
                pltpu.VMEM((HEAD_SIZE, seen), BF16),
                pltpu.VMEM((HEAD_SIZE, seen), BF16),
                pltpu.VMEM((seen, HEAD_SIZE), F32),
                pltpu.VMEM((seen, HEAD_SIZE), F32),
                pltpu.VMEM((seen, wide), F32),
                pltpu.VMEM((seen, wide), BF16),
                pltpu.VMEM((HEAD_SIZE, wide), F32),
                pltpu.VMEM((8, wide), F32),
                pltpu.VMEM((8, wide), F32),
            ],
        ),
        out_shape=[jax.ShapeDtypeStruct(q.shape, BF16)] * 2
        + [jax.ShapeDtypeStruct(shape, F32)]
        + [jax.ShapeDtypeStruct(shape, BF16)] * len(stores),
        input_output_aliases={before + n: n for n in range(len(carried))},
        compiler_params=pltpu.CompilerParams(vmem_limit_bytes=ATTEND_VMEM),
        cost_estimate=pl.CostEstimate(
            flops=count * 5 * 10**9, bytes_accessed=count << 22, transcendentals=count * 4 * tok * tok
        ),
        name="attend",
    )(starts, q, do, keys, values, *far_args, *carried)
    return results[:2], results[2], results[3:]


def combine_body(counts, *refs):
    k_ref, v_ref = refs[-2:]
    at = 0
    for g, number in enumerate(counts):
        total = refs[at][...]
        for n in range(1, number):
            total = total + refs[at + n][...].astype(F32)
        at += number
        columns = slice(g * HEAD_SIZE, (g + 1) * HEAD_SIZE)
        k_ref[:, columns] = total[:, :HEAD_SIZE].astype(BF16)
        v_ref[:, columns] = total[:, HEAD_SIZE:].astype(BF16)


def combine(heads):
    tok = heads[0][0][0].shape[0]
    terms = [term for head in heads for term in head]
    specs = [pl.BlockSpec((tok, 2 * HEAD_SIZE), lambda i, block=block: (0, block)) for _, block in terms]
    shape = (tok, len(heads) * HEAD_SIZE)
    return pl.pallas_call(
        functools.partial(combine_body, [len(head) for head in heads]),
        grid=(1,),
        in_specs=specs,
        out_specs=[pl.BlockSpec(shape, lambda i: (0, 0))] * 2,
        out_shape=[jax.ShapeDtypeStruct(shape, BF16)] * 2,
        compiler_params=pltpu.CompilerParams(vmem_limit_bytes=COMBINE_VMEM),
        cost_estimate=pl.CostEstimate(flops=1 << 20, bytes_accessed=2 << 20, transcendentals=0),
        name="combine",
    )(*[array for array, _ in terms])


def always(rank):
    return rank >= 0


def any_length(tok, reach, starts, queries, keys, values, output_cotangent):
    kv_heads = keys.shape[1] // HEAD_SIZE
    packed = jnp.concatenate([keys, values], 1)
    loads = [
        (from_behind(packed, dist), 0, kv_heads, (reach - dist) * tok, always) for dist in range(1, reach + 1)
    ]
    stores = [(reach - dist) * tok for dist in range(1, reach + 1)]
    outs, own, parts = attend(
        starts, queries, output_cotangent, keys, values, loads, stores, reach, 0, kv_heads
    )
    back = [from_behind(part, -dist) for dist, part in enumerate(parts, 1)]
    return (*outs, *combine([[(x, g) for x in (own, *back)] for g in range(kv_heads)]))


def two_halves(tok, starts, queries, keys, values, output_cotangent):
    kv_heads = keys.shape[1] // HEAD_SIZE
    near = lax.ppermute(jnp.concatenate([keys, values], 1), "seq", [(0, 1), (2, 3)])
    across_keys = 2 * tok - starts[0]
    across_queries = starts[1] - 2 * tok
    crossing = (across_keys > 0) & (across_queries > 0)
    plan = jnp.where(crossing, jnp.where(across_keys > tok, 2, 1), 0)

    def apart(near):
        outs, own, parts = attend(
            starts, queries, output_cotangent, keys, values, [(near, 0, kv_heads, 0, always)], [0], 1, 0, kv_heads
        )
        back = lax.ppermute(parts[0], "seq", [(1, 0), (3, 2)])
        return (*outs, *combine([[(own, g), (back, g)] for g in range(kv_heads)]))

    def across(long, near):
        packed = []
        for g in range(kv_heads):
            columns = slice(g * HEAD_SIZE, (g + 1) * HEAD_SIZE)
            packed.append(jnp.concatenate([keys[:, columns], values[:, columns]], 1))
        first = [lax.ppermute(x, "seq", [(1, 2)]) for x in packed]
        if long:
            second = [lax.ppermute(x, "seq", [(0, 2)]) for x in packed]
        else:
            second = [lax.ppermute(x, "seq", [(2, 3)]) for x in first]
        outs, terms, sent = (), [], ()
        for g in range(kv_heads):
            loads = [
                (near, g, kv_heads + g, tok, lambda rank: rank != 2),
                (first[g], 0, 1, tok, lambda rank: rank == 2),
                (second[g], 0, 1, 0, lambda rank: rank == (2 if long else 3)),
            ]
            outs, own, parts = attend(
                starts, queries, output_cotangent, keys, values, loads, [tok, 0], 2, g, 1, outs
            )
            parts = lax.optimization_barrier((*parts, *sent))[:2]
            sent = (
                lax.ppermute(parts[0], "seq", [(1, 0), (2, 1), (3, 2)]),
                lax.ppermute(parts[1], "seq", [(2, 0)] if long else [(3, 1)]),
            )
            terms.append([(own, 0), (sent[0], 0), (sent[1], 0)])
        return (*outs, *combine(terms))

    return lax.switch(plan, [apart, functools.partial(across, False), functools.partial(across, True)], near)


def on_device(queries, keys, values, doc_ids, output_cotangent):
    tok = keys.shape[0]
    count = lax.axis_size("seq")
    numbers = lax.broadcasted_iota(jnp.int32, (DOCS - 1, 1), 0)
    before = jnp.sum((doc_ids[None, :] <= numbers).astype(jnp.int32), axis=1)
    starts = lax.psum(before, "seq")
    span = min(WINDOW, tok * count // 2)
    reach = min((span + tok - 2) // tok, count - 1)
    if count == 4 and span == 2 * tok and tok % 512 == 0:
        return tuple(two_halves(tok, starts, queries, keys, values, output_cotangent))
    return any_length(tok, reach, starts, queries, keys, values, output_cotangent)


def solution(mesh):
    wide = P(("grp", "seq"), "head")
    in_specs = (wide, wide, wide, P(("grp", "seq")), wide)
    return jax.shard_map(
        on_device, mesh=mesh, in_specs=in_specs, out_specs=(wide,) * 4, check_vma=False
    )
```

```python
import functools
import math

import jax
import jax.numpy as jnp
from jax import lax
from jax.experimental import pallas as pl
from jax.experimental.pallas import tpu as pltpu
from jax.sharding import PartitionSpec as P

HEAD_SIZE = 128
WINDOW = 2048
DOCS = 3

NEG_FILL = -1e30
F32 = jnp.float32
BF16 = jnp.bfloat16
SCALE = 1.0 / math.sqrt(HEAD_SIZE)
LOG2_SCALE = math.log2(math.e) / math.sqrt(HEAD_SIZE)
SUM_ROWS = 16
COMBINE_VMEM = 12 << 20


def from_behind(value, steps):
    count = lax.axis_size("seq")
    first, last = (max(0, -steps), min(count, count - steps))
    return lax.ppermute(value, "seq", [(source, source + steps) for source in range(first, last)])


def dot(a, b, ca=1, cb=0):
    return lax.dot_general(a, b, (((ca,), (cb,)), ((), ())), preferred_element_type=F32)


def fold_rows(value, op):
    total = value[0:8]
    for j in range(8, value.shape[0], 8):
        total = op(total, value[j : j + 8])
    return total


def attend_body(tok, reach, group, tq, tk, loads, stores, carried, starts, q_ref, do_ref, own_k, own_v, *rest):
    far_in, rest = rest[: 2 * len(loads)], rest[2 * len(loads) + carried :]
    o_ref, dq_ref, own_ref = rest[:3]
    far_out, rest = rest[3 : 3 + len(stores)], rest[3 + len(stores) :]
    k_all, v_all, kt_all, vt_all, dk_all, dv_all, s_buf, e_buf, dp_buf, acc, top = rest
    tile, tiles = pl.program_id(1), pl.num_programs(1)
    rank = lax.axis_index("seq")
    start_1, start_2, q_first = starts[0], starts[1], rank * tok
    k_base = q_first - reach * tok
    q_pos = q_first + tile * tq
    heads = range(group)

    def first_live(i):
        doc_start = jnp.where(i < start_1, 0, jnp.where(i < start_2, start_1, start_2))
        return jnp.maximum(doc_start, i - (WINDOW - 1))

    def load(first, k_ref, v_ref):
        k, v = k_ref[...], v_ref[...]
        rows = slice(first, first + k.shape[0])
        k_all[rows, :], v_all[rows, :] = k, v
        kt_all[:, rows], vt_all[:HEAD_SIZE, rows] = k.T, v.T
        vt_all[HEAD_SIZE:, rows] = jnp.ones((SUM_ROWS, k.shape[0]), BF16)
        dk_all[rows, :] = jnp.zeros(k.shape, F32)
        dv_all[rows, :] = jnp.zeros(v.shape, F32)

    @pl.when(tile == 0)
    def _():
        needed = first_live(q_first) - k_base
        load(reach * tok, own_k, own_v)
        for n, (first, when) in enumerate(loads):
            k_ref, v_ref = far_in[2 * n : 2 * n + 2]
            pl.when(when(rank) & (needed < first + k_ref.shape[0]))(functools.partial(load, first, k_ref, v_ref))

    low = jnp.maximum(first_live(q_pos) - k_base, 0) // tk
    high = (q_pos + tq - 1 - k_base) // tk + 1
    last_first = first_live(q_pos + tq - 1)

    def one_by_one(visit):
        def one(n, carry):
            visit(pl.multiple_of(n * tk, tk), tk)
            return carry

        lax.fori_loop(low, high, one, 0)

    def over_keys(visit):
        def two(n, carry):
            visit(pl.multiple_of((low + 2 * n) * tk, tk), 2 * tk)
            return carry

        lax.fori_loop(0, (high - low) // 2, two, 0)

        @pl.when((high - low) % 2 == 1)
        def _():
            visit(pl.multiple_of((high - 1) * tk, tk), tk)

    q = jnp.concatenate([q_ref[:, h * HEAD_SIZE : (h + 1) * HEAD_SIZE] for h in heads], 0)
    do_t = jnp.concatenate([do_ref[:, h * HEAD_SIZE : (h + 1) * HEAD_SIZE].T for h in heads], 1)
    top[...] = jnp.full_like(top, NEG_FILL)

    def scores(off, size):
        s = dot(k_all[pl.ds(off, size), :], q, 1, 1)
        k_pos = k_base + off
        full = (k_pos >= last_first) & (k_pos + size - 1 <= q_pos)

        def put(s):
            s_buf[pl.ds(off, size), :] = s
            top[...] = jnp.maximum(top[...], fold_rows(s, jnp.maximum))

        @pl.when(full)
        def _():
            put(s)

        @pl.when(jnp.logical_not(full))
        def _():
            j = k_pos + lax.broadcasted_iota(jnp.int32, (size, tq), 0)
            i = q_pos + lax.broadcasted_iota(jnp.int32, (size, tq), 1)
            first = first_live(q_pos + lax.broadcasted_iota(jnp.int32, (1, tq), 1))
            live = (j <= i) & (j >= first)
            put(jnp.concatenate([jnp.where(live, s[:, h * tq : (h + 1) * tq], NEG_FILL) for h in heads], 1))

    one_by_one(scores)
    m = jnp.max(top[...], axis=0, keepdims=True)
    acc[...] = jnp.zeros_like(acc)

    def weigh(off, size):
        keys = pl.ds(off, size)
        dp_buf[keys, :] = dot(v_all[keys, :], do_t)
        eb = jnp.exp2((s_buf[keys, :] - m) * LOG2_SCALE).astype(BF16)
        e_buf[keys, :] = eb
        acc[...] += dot(vt_all[:, keys], eb)

    over_keys(weigh)
    inverse = 1.0 / acc[HEAD_SIZE : HEAD_SIZE + 1, :]
    out_t = (acc[:HEAD_SIZE, :] * inverse).astype(BF16)
    for h in heads:
        o_ref[:, h * HEAD_SIZE : (h + 1) * HEAD_SIZE] = out_t[:, h * tq : (h + 1) * tq].T
    delta = jnp.sum(do_t.astype(F32) * out_t.astype(F32), axis=0, keepdims=True) * inverse
    scaled_t = (do_t.astype(F32) * inverse).astype(BF16)
    scaled = jnp.concatenate([scaled_t[:, h * tq : (h + 1) * tq].T for h in heads], 0)
    acc[...] = jnp.zeros_like(acc)

    def back(off, size):
        keys = pl.ds(off, size)
        eb = e_buf[keys, :]
        dv_all[keys, :] += dot(eb, scaled)
        ds = (eb.astype(F32) * (dp_buf[keys, :] * inverse - delta)).astype(BF16)
        dk_all[keys, :] += dot(ds, q)
        acc[:HEAD_SIZE, :] += dot(kt_all[:, keys], ds)

    over_keys(back)
    dq_t = (acc[:HEAD_SIZE, :] * SCALE).astype(BF16)
    for h in heads:
        dq_ref[:, h * HEAD_SIZE : (h + 1) * HEAD_SIZE] = dq_t[:, h * tq : (h + 1) * tq].T

    @pl.when(tile == tiles - 1)
    def _():
        needed = first_live(q_first) - k_base
        own_ref[:, :HEAD_SIZE] = dk_all[reach * tok :, :] * SCALE
        own_ref[:, HEAD_SIZE:] = dv_all[reach * tok :, :]
        for ref, row in zip(far_out, stores):
            rows = slice(row, row + ref.shape[0])

            @pl.when(needed < row + ref.shape[0])
            def _(ref=ref, rows=rows):
                ref[:, :HEAD_SIZE] = (dk_all[rows, :] * SCALE).astype(BF16)
                ref[:, HEAD_SIZE:] = dv_all[rows, :].astype(BF16)

            @pl.when(needed >= row + ref.shape[0])
            def _(ref=ref):
                ref[...] = jnp.zeros_like(ref)


def attend(starts, q, do, keys, values, loads, stores, reach, first_head, count, carried=()):
    tok = q.shape[0]
    group = q.shape[1] // keys.shape[1]
    tq = tk = min(256, tok)
    wide = group * tq
    seen = (reach + 1) * tok
    q_spec = pl.BlockSpec((tq, group * HEAD_SIZE), lambda g, i, s: (i, g + first_head))

    def kv_spec(rows, first):
        return pl.BlockSpec((rows, HEAD_SIZE), lambda g, i, s, first=first: (0, g + first))

    far_args, far_specs = [], []
    for array, k_block, v_block, _, _ in loads:
        far_args += [array, array]
        far_specs += [kv_spec(array.shape[0], k_block), kv_spec(array.shape[0], v_block)]
    part = pl.BlockSpec((tok, 2 * HEAD_SIZE), lambda g, i, s: (0, g))
    shape = (tok, 2 * count * HEAD_SIZE)
    before = 5 + len(far_args)
    results = pl.pallas_call(
        functools.partial(
            attend_body, tok, reach, group, tq, tk, [load[3:] for load in loads], stores, len(carried)
        ),
        grid_spec=pltpu.PrefetchScalarGridSpec(
            num_scalar_prefetch=1,
            grid=(count, tok // tq),
            in_specs=[q_spec, q_spec, kv_spec(tok, first_head), kv_spec(tok, first_head)]
            + far_specs
            + [pl.BlockSpec(memory_space=pl.ANY)] * len(carried),
            out_specs=[q_spec, q_spec] + [part] * (1 + len(stores)),
            scratch_shapes=[
                pltpu.VMEM((seen, HEAD_SIZE), BF16),
                pltpu.VMEM((seen, HEAD_SIZE), BF16),
                pltpu.VMEM((HEAD_SIZE, seen), BF16),
                pltpu.VMEM((HEAD_SIZE + SUM_ROWS, seen), BF16),
                pltpu.VMEM((seen, HEAD_SIZE), F32),
                pltpu.VMEM((seen, HEAD_SIZE), F32),
                pltpu.VMEM((seen, wide), F32),
                pltpu.VMEM((seen, wide), BF16),
                pltpu.VMEM((seen, wide), F32),
                pltpu.VMEM((HEAD_SIZE + SUM_ROWS, wide), F32),
                pltpu.VMEM((8, wide), F32),
            ],
        ),
        out_shape=[jax.ShapeDtypeStruct(q.shape, BF16)] * 2
        + [jax.ShapeDtypeStruct(shape, F32)]
        + [jax.ShapeDtypeStruct(shape, BF16)] * len(stores),
        input_output_aliases={before + n: n for n in range(len(carried))},
        compiler_params=pltpu.CompilerParams(vmem_limit_bytes=(12 << 20) + 10 * seen * wide),
        cost_estimate=pl.CostEstimate(
            flops=count * 5 * 10**9, bytes_accessed=count << 22, transcendentals=count * 4 * tok * tok
        ),
        name="attend",
    )(starts, q, do, keys, values, *far_args, *carried)
    return results[:2], results[2], results[3:]


def combine_body(counts, *refs):
    k_ref, v_ref = refs[-2:]
    at = 0
    for g, number in enumerate(counts):
        total = refs[at][...]
        for n in range(1, number):
            total = total + refs[at + n][...].astype(F32)
        at += number
        columns = slice(g * HEAD_SIZE, (g + 1) * HEAD_SIZE)
        k_ref[:, columns] = total[:, :HEAD_SIZE].astype(BF16)
        v_ref[:, columns] = total[:, HEAD_SIZE:].astype(BF16)


def combine(heads):
    tok = heads[0][0][0].shape[0]
    terms = [term for head in heads for term in head]
    specs = [pl.BlockSpec((tok, 2 * HEAD_SIZE), lambda i, block=block: (0, block)) for _, block in terms]
    shape = (tok, len(heads) * HEAD_SIZE)
    return pl.pallas_call(
        functools.partial(combine_body, [len(head) for head in heads]),
        grid=(1,),
        in_specs=specs,
        out_specs=[pl.BlockSpec(shape, lambda i: (0, 0))] * 2,
        out_shape=[jax.ShapeDtypeStruct(shape, BF16)] * 2,
        compiler_params=pltpu.CompilerParams(vmem_limit_bytes=COMBINE_VMEM),
        cost_estimate=pl.CostEstimate(flops=1 << 20, bytes_accessed=2 << 20, transcendentals=0),
        name="combine",
    )(*[array for array, _ in terms])


def always(rank):
    return rank >= 0


def any_length(tok, reach, starts, queries, keys, values, output_cotangent):
    kv_heads = keys.shape[1] // HEAD_SIZE
    packed = jnp.concatenate([keys, values], 1)
    loads = [
        (from_behind(packed, dist), 0, kv_heads, (reach - dist) * tok, always) for dist in range(1, reach + 1)
    ]
    stores = [(reach - dist) * tok for dist in range(1, reach + 1)]
    outs, own, parts = attend(
        starts, queries, output_cotangent, keys, values, loads, stores, reach, 0, kv_heads
    )
    back = [from_behind(part, -dist) for dist, part in enumerate(parts, 1)]
    return (*outs, *combine([[(x, g) for x in (own, *back)] for g in range(kv_heads)]))


def two_halves(tok, starts, queries, keys, values, output_cotangent):
    kv_heads = keys.shape[1] // HEAD_SIZE
    near = lax.ppermute(jnp.concatenate([keys, values], 1), "seq", [(0, 1), (2, 3)])
    across_keys = 2 * tok - starts[0]
    across_queries = starts[1] - 2 * tok
    crossing = (across_keys > 0) & (across_queries > 0)
    plan = jnp.where(crossing, jnp.where(across_keys > tok, 2, 1), 0)

    def apart(near):
        outs, own, parts = attend(
            starts, queries, output_cotangent, keys, values, [(near, 0, kv_heads, 0, always)], [0], 1, 0, kv_heads
        )
        back = lax.ppermute(parts[0], "seq", [(1, 0), (3, 2)])
        return (*outs, *combine([[(own, g), (back, g)] for g in range(kv_heads)]))

    def across(long, near):
        packed = []
        for g in range(kv_heads):
            columns = slice(g * HEAD_SIZE, (g + 1) * HEAD_SIZE)
            packed.append(jnp.concatenate([keys[:, columns], values[:, columns]], 1))
        first = [lax.ppermute(x, "seq", [(1, 2)]) for x in packed]
        if long:
            second = [lax.ppermute(x, "seq", [(0, 2)]) for x in packed]
        else:
            second = [lax.ppermute(x, "seq", [(2, 3)]) for x in first]
        outs, terms, sent = (), [], ()
        for g in range(kv_heads):
            loads = [
                (near, g, kv_heads + g, tok, lambda rank: rank != 2),
                (first[g], 0, 1, tok, lambda rank: rank == 2),
                (second[g], 0, 1, 0, lambda rank: rank == (2 if long else 3)),
            ]
            outs, own, parts = attend(
                starts, queries, output_cotangent, keys, values, loads, [tok, 0], 2, g, 1, outs
            )
            parts = lax.optimization_barrier((*parts, *sent))[:2]
            sent = (
                lax.ppermute(parts[0], "seq", [(1, 0), (2, 1), (3, 2)]),
                lax.ppermute(parts[1], "seq", [(2, 0)] if long else [(3, 1)]),
            )
            terms.append([(own, 0), (sent[0], 0), (sent[1], 0)])
        return (*outs, *combine(terms))

    return lax.switch(plan, [apart, functools.partial(across, False), functools.partial(across, True)], near)


def on_device(queries, keys, values, doc_ids, output_cotangent):
    tok = keys.shape[0]
    count = lax.axis_size("seq")
    numbers = lax.broadcasted_iota(jnp.int32, (DOCS - 1, 1), 0)
    before = jnp.sum((doc_ids[None, :] <= numbers).astype(jnp.int32), axis=1)
    starts = lax.psum(before, "seq")
    span = min(WINDOW, tok * count // 2)
    reach = min((span + tok - 2) // tok, count - 1)
    if count == 4 and span == 2 * tok and tok % 512 == 0:
        return tuple(two_halves(tok, starts, queries, keys, values, output_cotangent))
    return any_length(tok, reach, starts, queries, keys, values, output_cotangent)


def solution(mesh):
    wide = P(("grp", "seq"), "head")
    in_specs = (wide, wide, wide, P(("grp", "seq")), wide)
    return jax.shard_map(
        on_device, mesh=mesh, in_specs=in_specs, out_specs=(wide,) * 4, check_vma=False
    )
```

```python
import functools
import math

import jax
import jax.numpy as jnp
from jax import lax
from jax.experimental import pallas as pl
from jax.experimental.pallas import tpu as pltpu
from jax.sharding import PartitionSpec as P

HEAD_SIZE = 128
WINDOW = 2048
DOCS = 3

NEG_FILL = -1e30
F32 = jnp.float32
BF16 = jnp.bfloat16
SCALE = 1.0 / math.sqrt(HEAD_SIZE)
LOG2_SCALE = math.log2(math.e) / math.sqrt(HEAD_SIZE)
SUM_ROWS = 16
COMBINE_VMEM = 12 << 20


def from_behind(value, steps):
    count = lax.axis_size("seq")
    first, last = (max(0, -steps), min(count, count - steps))
    return lax.ppermute(value, "seq", [(source, source + steps) for source in range(first, last)])


def dot(a, b, ca=1, cb=0):
    return lax.dot_general(a, b, (((ca,), (cb,)), ((), ())), preferred_element_type=F32)


def fold_rows(value, op):
    total = value[0:8]
    for j in range(8, value.shape[0], 8):
        total = op(total, value[j : j + 8])
    return total


def attend_body(tok, reach, group, tq, tk, loads, stores, carried, starts, q_ref, do_ref, own_k, own_v, *rest):
    far_in, rest = rest[: 2 * len(loads)], rest[2 * len(loads) + carried :]
    o_ref, dq_ref, own_ref = rest[:3]
    far_out, rest = rest[3 : 3 + len(stores)], rest[3 + len(stores) :]
    k_all, v_all, kt_all, vt_all, dk_all, dv_all, s_buf, e_buf, dp_buf, acc, top = rest
    tile, tiles = pl.program_id(1), pl.num_programs(1)
    rank = lax.axis_index("seq")
    start_1, start_2, q_first = starts[0], starts[1], rank * tok
    k_base = q_first - reach * tok
    q_pos = q_first + tile * tq
    heads = range(group)

    def first_live(i):
        doc_start = jnp.where(i < start_1, 0, jnp.where(i < start_2, start_1, start_2))
        return jnp.maximum(doc_start, i - (WINDOW - 1))

    def load(first, k_ref, v_ref):
        k, v = k_ref[...], v_ref[...]
        rows = slice(first, first + k.shape[0])
        k_all[rows, :], v_all[rows, :] = k, v
        kt_all[:, rows], vt_all[:HEAD_SIZE, rows] = k.T, v.T
        vt_all[HEAD_SIZE:, rows] = jnp.ones((SUM_ROWS, k.shape[0]), BF16)
        dk_all[rows, :] = jnp.zeros(k.shape, F32)
        dv_all[rows, :] = jnp.zeros(v.shape, F32)

    @pl.when(tile == 0)
    def _():
        needed = first_live(q_first) - k_base
        load(reach * tok, own_k, own_v)
        for n, (first, when) in enumerate(loads):
            k_ref, v_ref = far_in[2 * n : 2 * n + 2]
            pl.when(when(rank) & (needed < first + k_ref.shape[0]))(functools.partial(load, first, k_ref, v_ref))

    low = jnp.maximum(first_live(q_pos) - k_base, 0) // tk
    units = (q_pos + tq - k_base) // tk - low
    last_first = first_live(q_pos + tq - 1)

    def over_keys(visit, most):
        def run(n, carry):
            visit(pl.multiple_of((low + most * n) * tk, tk), most * tk)
            return carry

        lax.fori_loop(0, units // most, run, 0)
        size = most // 2
        while size:

            @pl.when(units % (2 * size) >= size)
            def _(size=size):
                visit(pl.multiple_of((low + units // (2 * size) * (2 * size)) * tk, tk), size * tk)

            size //= 2

    q = jnp.concatenate([q_ref[:, h * HEAD_SIZE : (h + 1) * HEAD_SIZE] for h in heads], 0)
    do_t = jnp.concatenate([do_ref[:, h * HEAD_SIZE : (h + 1) * HEAD_SIZE].T for h in heads], 1)
    top[...] = jnp.full_like(top, NEG_FILL)

    def scores(off, size):
        s = dot(k_all[pl.ds(off, size), :], q, 1, 1)
        k_pos = k_base + off
        full = (k_pos >= last_first) & (k_pos + size - 1 <= q_pos)

        def put(s):
            s_buf[pl.ds(off, size), :] = s
            top[...] = jnp.maximum(top[...], fold_rows(s, jnp.maximum))

        @pl.when(full)
        def _():
            put(s)

        @pl.when(jnp.logical_not(full))
        def _():
            j = k_pos + lax.broadcasted_iota(jnp.int32, (size, tq), 0)
            i = q_pos + lax.broadcasted_iota(jnp.int32, (size, tq), 1)
            first = first_live(q_pos + lax.broadcasted_iota(jnp.int32, (1, tq), 1))
            live = (j <= i) & (j >= first)
            put(jnp.concatenate([jnp.where(live, s[:, h * tq : (h + 1) * tq], NEG_FILL) for h in heads], 1))

    over_keys(scores, 2)
    m = jnp.max(top[...], axis=0, keepdims=True)
    acc[...] = jnp.zeros_like(acc)

    def weigh(off, size):
        keys = pl.ds(off, size)
        dp_buf[keys, :] = dot(v_all[keys, :], do_t)
        eb = jnp.exp2((s_buf[keys, :] - m) * LOG2_SCALE).astype(BF16)
        e_buf[keys, :] = eb
        acc[...] += dot(vt_all[:, keys], eb)

    over_keys(weigh, 4)
    inverse = 1.0 / acc[HEAD_SIZE : HEAD_SIZE + 1, :]
    out_t = (acc[:HEAD_SIZE, :] * inverse).astype(BF16)
    for h in heads:
        o_ref[:, h * HEAD_SIZE : (h + 1) * HEAD_SIZE] = out_t[:, h * tq : (h + 1) * tq].T
    delta = jnp.sum(do_t.astype(F32) * out_t.astype(F32), axis=0, keepdims=True) * inverse
    scaled_t = (do_t.astype(F32) * inverse).astype(BF16)
    scaled = jnp.concatenate([scaled_t[:, h * tq : (h + 1) * tq].T for h in heads], 0)
    acc[...] = jnp.zeros_like(acc)

    def back(off, size):
        keys = pl.ds(off, size)
        eb = e_buf[keys, :]
        dv_all[keys, :] += dot(eb, scaled)
        ds = (eb.astype(F32) * (dp_buf[keys, :] * inverse - delta)).astype(BF16)
        dk_all[keys, :] += dot(ds, q)
        acc[:HEAD_SIZE, :] += dot(kt_all[:, keys], ds)

    over_keys(back, 4)
    dq_t = (acc[:HEAD_SIZE, :] * SCALE).astype(BF16)
    for h in heads:
        dq_ref[:, h * HEAD_SIZE : (h + 1) * HEAD_SIZE] = dq_t[:, h * tq : (h + 1) * tq].T

    @pl.when(tile == tiles - 1)
    def _():
        needed = first_live(q_first) - k_base
        own_ref[:, :HEAD_SIZE] = dk_all[reach * tok :, :] * SCALE
        own_ref[:, HEAD_SIZE:] = dv_all[reach * tok :, :]
        for ref, row in zip(far_out, stores):
            rows = slice(row, row + ref.shape[0])

            @pl.when(needed < row + ref.shape[0])
            def _(ref=ref, rows=rows):
                ref[:, :HEAD_SIZE] = (dk_all[rows, :] * SCALE).astype(BF16)
                ref[:, HEAD_SIZE:] = dv_all[rows, :].astype(BF16)

            @pl.when(needed >= row + ref.shape[0])
            def _(ref=ref):
                ref[...] = jnp.zeros_like(ref)


def attend(starts, q, do, keys, values, loads, stores, reach, first_head, count, carried=()):
    tok = q.shape[0]
    group = q.shape[1] // keys.shape[1]
    tq, tk = min(256, tok), min(128, tok)
    wide = group * tq
    seen = (reach + 1) * tok
    q_spec = pl.BlockSpec((tq, group * HEAD_SIZE), lambda g, i, s: (i, g + first_head))

    def kv_spec(rows, first):
        return pl.BlockSpec((rows, HEAD_SIZE), lambda g, i, s, first=first: (0, g + first))

    far_args, far_specs = [], []
    for array, k_block, v_block, _, _ in loads:
        far_args += [array, array]
        far_specs += [kv_spec(array.shape[0], k_block), kv_spec(array.shape[0], v_block)]
    part = pl.BlockSpec((tok, 2 * HEAD_SIZE), lambda g, i, s: (0, g))
    shape = (tok, 2 * count * HEAD_SIZE)
    before = 5 + len(far_args)
    results = pl.pallas_call(
        functools.partial(
            attend_body, tok, reach, group, tq, tk, [load[3:] for load in loads], stores, len(carried)
        ),
        grid_spec=pltpu.PrefetchScalarGridSpec(
            num_scalar_prefetch=1,
            grid=(count, tok // tq),
            in_specs=[q_spec, q_spec, kv_spec(tok, first_head), kv_spec(tok, first_head)]
            + far_specs
            + [pl.BlockSpec(memory_space=pl.ANY)] * len(carried),
            out_specs=[q_spec, q_spec] + [part] * (1 + len(stores)),
            scratch_shapes=[
                pltpu.VMEM((seen, HEAD_SIZE), BF16),
                pltpu.VMEM((seen, HEAD_SIZE), BF16),
                pltpu.VMEM((HEAD_SIZE, seen), BF16),
                pltpu.VMEM((HEAD_SIZE + SUM_ROWS, seen), BF16),
                pltpu.VMEM((seen, HEAD_SIZE), F32),
                pltpu.VMEM((seen, HEAD_SIZE), F32),
                pltpu.VMEM((seen, wide), F32),
                pltpu.VMEM((seen, wide), BF16),
                pltpu.VMEM((seen, wide), F32),
                pltpu.VMEM((HEAD_SIZE + SUM_ROWS, wide), F32),
                pltpu.VMEM((8, wide), F32),
            ],
        ),
        out_shape=[jax.ShapeDtypeStruct(q.shape, BF16)] * 2
        + [jax.ShapeDtypeStruct(shape, F32)]
        + [jax.ShapeDtypeStruct(shape, BF16)] * len(stores),
        input_output_aliases={before + n: n for n in range(len(carried))},
        compiler_params=pltpu.CompilerParams(vmem_limit_bytes=(12 << 20) + 10 * seen * wide),
        cost_estimate=pl.CostEstimate(
            flops=count * 5 * 10**9, bytes_accessed=count << 22, transcendentals=count * 4 * tok * tok
        ),
        name="attend",
    )(starts, q, do, keys, values, *far_args, *carried)
    return results[:2], results[2], results[3:]


def combine_body(counts, *refs):
    k_ref, v_ref = refs[-2:]
    at = 0
    for g, number in enumerate(counts):
        total = refs[at][...]
        for n in range(1, number):
            total = total + refs[at + n][...].astype(F32)
        at += number
        columns = slice(g * HEAD_SIZE, (g + 1) * HEAD_SIZE)
        k_ref[:, columns] = total[:, :HEAD_SIZE].astype(BF16)
        v_ref[:, columns] = total[:, HEAD_SIZE:].astype(BF16)


def combine(heads):
    tok = heads[0][0][0].shape[0]
    terms = [term for head in heads for term in head]
    specs = [pl.BlockSpec((tok, 2 * HEAD_SIZE), lambda i, block=block: (0, block)) for _, block in terms]
    shape = (tok, len(heads) * HEAD_SIZE)
    return pl.pallas_call(
        functools.partial(combine_body, [len(head) for head in heads]),
        grid=(1,),
        in_specs=specs,
        out_specs=[pl.BlockSpec(shape, lambda i: (0, 0))] * 2,
        out_shape=[jax.ShapeDtypeStruct(shape, BF16)] * 2,
        compiler_params=pltpu.CompilerParams(vmem_limit_bytes=COMBINE_VMEM),
        cost_estimate=pl.CostEstimate(flops=1 << 20, bytes_accessed=2 << 20, transcendentals=0),
        name="combine",
    )(*[array for array, _ in terms])


def always(rank):
    return rank >= 0


def any_length(tok, reach, starts, queries, keys, values, output_cotangent):
    kv_heads = keys.shape[1] // HEAD_SIZE
    packed = jnp.concatenate([keys, values], 1)
    loads = [
        (from_behind(packed, dist), 0, kv_heads, (reach - dist) * tok, always) for dist in range(1, reach + 1)
    ]
    stores = [(reach - dist) * tok for dist in range(1, reach + 1)]
    outs, own, parts = attend(
        starts, queries, output_cotangent, keys, values, loads, stores, reach, 0, kv_heads
    )
    back = [from_behind(part, -dist) for dist, part in enumerate(parts, 1)]
    return (*outs, *combine([[(x, g) for x in (own, *back)] for g in range(kv_heads)]))


def two_halves(tok, starts, queries, keys, values, output_cotangent):
    kv_heads = keys.shape[1] // HEAD_SIZE
    near = lax.ppermute(jnp.concatenate([keys, values], 1), "seq", [(0, 1), (2, 3)])
    across_keys = 2 * tok - starts[0]
    across_queries = starts[1] - 2 * tok
    crossing = (across_keys > 0) & (across_queries > 0)
    plan = jnp.where(crossing, jnp.where(across_keys > tok, 2, 1), 0)

    def apart(near):
        outs, own, parts = attend(
            starts, queries, output_cotangent, keys, values, [(near, 0, kv_heads, 0, always)], [0], 1, 0, kv_heads
        )
        back = lax.ppermute(parts[0], "seq", [(1, 0), (3, 2)])
        return (*outs, *combine([[(own, g), (back, g)] for g in range(kv_heads)]))

    def across(long, near):
        packed = []
        for g in range(kv_heads):
            own = [x[:, g * HEAD_SIZE : (g + 1) * HEAD_SIZE] for x in (keys, values)]
            block = jnp.concatenate(own, 1)
            if long:
                at = [x * HEAD_SIZE for x in (g, kv_heads + g)]
                behind = jnp.concatenate([near[:, x : x + HEAD_SIZE] for x in at], 1)
                block = jnp.concatenate([behind, block], 0)
            packed.append(block)
        first = [lax.ppermute(x, "seq", [(1, 2)]) for x in packed]
        if not long:
            second = [lax.ppermute(x, "seq", [(2, 3)]) for x in first]
        outs, terms, sent = (), [], ()
        for g in range(kv_heads):
            loads = [
                (near, g, kv_heads + g, tok, lambda rank: rank != 2),
                (first[g], 0, 1, 0 if long else tok, lambda rank: rank == 2),
            ]
            if not long:
                loads.append((second[g], 0, 1, 0, lambda rank: rank == 3))
            outs, own, parts = attend(
                starts, queries, output_cotangent, keys, values, loads, [tok, 0], 2, g, 1, outs
            )
            parts = lax.optimization_barrier((*parts, *sent))[:2]
            sent = (
                lax.ppermute(parts[0], "seq", [(1, 0), (2, 1), (3, 2)]),
                lax.ppermute(parts[1], "seq", [(2, 0)] if long else [(3, 1)]),
            )
            terms.append([(own, 0), (sent[0], 0), (sent[1], 0)])
        return (*outs, *combine(terms))

    return lax.switch(plan, [apart, functools.partial(across, False), functools.partial(across, True)], near)


def on_device(queries, keys, values, doc_ids, output_cotangent):
    tok = keys.shape[0]
    count = lax.axis_size("seq")
    numbers = lax.broadcasted_iota(jnp.int32, (DOCS - 1, 1), 0)
    before = jnp.sum((doc_ids[None, :] <= numbers).astype(jnp.int32), axis=1)
    starts = lax.psum(before, "seq")
    span = min(WINDOW, tok * count // 2)
    reach = min((span + tok - 2) // tok, count - 1)
    if count == 4 and span == 2 * tok and tok % 512 == 0:
        return tuple(two_halves(tok, starts, queries, keys, values, output_cotangent))
    return any_length(tok, reach, starts, queries, keys, values, output_cotangent)


def solution(mesh):
    wide = P(("grp", "seq"), "head")
    in_specs = (wide, wide, wide, P(("grp", "seq")), wide)
    return jax.shard_map(
        on_device, mesh=mesh, in_specs=in_specs, out_specs=(wide,) * 4, check_vma=False
    )
```

```python
import functools
import math

import jax
import jax.numpy as jnp
from jax import lax
from jax.experimental import pallas as pl
from jax.experimental.pallas import tpu as pltpu
from jax.sharding import PartitionSpec as P

HEAD_SIZE = 128
WINDOW = 2048
DOCS = 3

NEG_FILL = -1e30
F32 = jnp.float32
BF16 = jnp.bfloat16
SCALE = 1.0 / math.sqrt(HEAD_SIZE)
LOG2_SCALE = math.log2(math.e) / math.sqrt(HEAD_SIZE)
SUM_ROWS = 16
COMBINE_VMEM = 12 << 20


def from_behind(value, steps):
    count = lax.axis_size("seq")
    first, last = (max(0, -steps), min(count, count - steps))
    return lax.ppermute(value, "seq", [(source, source + steps) for source in range(first, last)])


def dot(a, b, ca=1, cb=0):
    return lax.dot_general(a, b, (((ca,), (cb,)), ((), ())), preferred_element_type=F32)


def fold_rows(value, op):
    total = value[0:8]
    for j in range(8, value.shape[0], 8):
        total = op(total, value[j : j + 8])
    return total


def attend_body(tok, reach, group, tq, tk, loads, stores, carried, starts, q_ref, do_ref, own_k, own_v, *rest):
    far_in, rest = rest[: 2 * len(loads)], rest[2 * len(loads) + carried :]
    o_ref, dq_ref, own_ref = rest[:3]
    far_out, rest = rest[3 : 3 + len(stores)], rest[3 + len(stores) :]
    k_all, v_all, kt_all, vt_all, dk_all, dv_all, s_buf, e_buf, dp_buf, acc, top = rest
    tile, tiles = pl.program_id(1), pl.num_programs(1)
    rank = lax.axis_index("seq")
    start_1, start_2, q_first = starts[0], starts[1], rank * tok
    k_base = q_first - reach * tok
    q_pos = q_first + tile * tq
    heads = range(group)

    def first_live(i):
        doc_start = jnp.where(i < start_1, 0, jnp.where(i < start_2, start_1, start_2))
        return jnp.maximum(doc_start, i - (WINDOW - 1))

    def load(first, k_ref, v_ref):
        k, v = k_ref[...], v_ref[...]
        rows = slice(first, first + k.shape[0])
        k_all[rows, :], v_all[rows, :] = k, v
        kt_all[:, rows], vt_all[:HEAD_SIZE, rows] = k.T, v.T
        vt_all[HEAD_SIZE:, rows] = jnp.ones((SUM_ROWS, k.shape[0]), BF16)
        dk_all[rows, :] = jnp.zeros(k.shape, F32)
        dv_all[rows, :] = jnp.zeros(v.shape, F32)

    @pl.when(tile == 0)
    def _():
        needed = first_live(q_first) - k_base
        load(reach * tok, own_k, own_v)
        for n, (first, when) in enumerate(loads):
            k_ref, v_ref = far_in[2 * n : 2 * n + 2]
            pl.when(when(rank) & (needed < first + k_ref.shape[0]))(functools.partial(load, first, k_ref, v_ref))

    low = jnp.maximum(first_live(q_pos) - k_base, 0) // tk
    units = (q_pos + tq - k_base) // tk - low
    last_first = first_live(q_pos + tq - 1)

    def over_keys(visit, most):
        def run(n, carry):
            visit(pl.multiple_of((low + most * n) * tk, tk), most * tk)
            return carry

        lax.fori_loop(0, units // most, run, 0)
        size = most // 2
        while size:

            @pl.when(units % (2 * size) >= size)
            def _(size=size):
                visit(pl.multiple_of((low + units // (2 * size) * (2 * size)) * tk, tk), size * tk)

            size //= 2

    q = jnp.concatenate([q_ref[:, h * HEAD_SIZE : (h + 1) * HEAD_SIZE] for h in heads], 0)
    do_t = jnp.concatenate([do_ref[:, h * HEAD_SIZE : (h + 1) * HEAD_SIZE].T for h in heads], 1)
    top[...] = jnp.full_like(top, NEG_FILL)

    def scores(off, size):
        s = dot(k_all[pl.ds(off, size), :], q, 1, 1)
        k_pos = k_base + off
        full = (k_pos >= last_first) & (k_pos + size - 1 <= q_pos)

        def put(s):
            s_buf[pl.ds(off, size), :] = s
            top[...] = jnp.maximum(top[...], fold_rows(s, jnp.maximum))

        @pl.when(full)
        def _():
            put(s)

        @pl.when(jnp.logical_not(full))
        def _():
            j = k_pos + lax.broadcasted_iota(jnp.int32, (size, tq), 0)
            i = q_pos + lax.broadcasted_iota(jnp.int32, (size, tq), 1)
            first = first_live(q_pos + lax.broadcasted_iota(jnp.int32, (1, tq), 1))
            live = (j <= i) & (j >= first)
            put(jnp.concatenate([jnp.where(live, s[:, h * tq : (h + 1) * tq], NEG_FILL) for h in heads], 1))

    over_keys(scores, 4)
    m = jnp.max(top[...], axis=0, keepdims=True)
    acc[...] = jnp.zeros_like(acc)

    def weigh(off, size):
        keys = pl.ds(off, size)
        dp_buf[keys, :] = dot(v_all[keys, :], do_t)
        eb = jnp.exp2((s_buf[keys, :] - m) * LOG2_SCALE).astype(BF16)
        e_buf[keys, :] = eb
        acc[...] += dot(vt_all[:, keys], eb)

    over_keys(weigh, 4)
    inverse = 1.0 / acc[HEAD_SIZE : HEAD_SIZE + 1, :]
    out_t = (acc[:HEAD_SIZE, :] * inverse).astype(BF16)
    for h in heads:
        o_ref[:, h * HEAD_SIZE : (h + 1) * HEAD_SIZE] = out_t[:, h * tq : (h + 1) * tq].T
    delta = jnp.sum(do_t.astype(F32) * out_t.astype(F32), axis=0, keepdims=True) * inverse
    scaled_t = (do_t.astype(F32) * inverse).astype(BF16)
    scaled = jnp.concatenate([scaled_t[:, h * tq : (h + 1) * tq].T for h in heads], 0)
    acc[...] = jnp.zeros_like(acc)

    def back(off, size):
        keys = pl.ds(off, size)
        eb = e_buf[keys, :]
        dv_all[keys, :] += dot(eb, scaled)
        ds = (eb.astype(F32) * (dp_buf[keys, :] * inverse - delta)).astype(BF16)
        dk_all[keys, :] += dot(ds, q)
        acc[:HEAD_SIZE, :] += dot(kt_all[:, keys], ds)

    over_keys(back, 4)
    dq_t = (acc[:HEAD_SIZE, :] * SCALE).astype(BF16)
    for h in heads:
        dq_ref[:, h * HEAD_SIZE : (h + 1) * HEAD_SIZE] = dq_t[:, h * tq : (h + 1) * tq].T

    @pl.when(tile == tiles - 1)
    def _():
        needed = first_live(q_first) - k_base
        own_ref[:, :HEAD_SIZE] = dk_all[reach * tok :, :] * SCALE
        own_ref[:, HEAD_SIZE:] = dv_all[reach * tok :, :]
        for ref, row in zip(far_out, stores):
            rows = slice(row, row + ref.shape[0])

            @pl.when(needed < row + ref.shape[0])
            def _(ref=ref, rows=rows):
                ref[:, :HEAD_SIZE] = (dk_all[rows, :] * SCALE).astype(BF16)
                ref[:, HEAD_SIZE:] = dv_all[rows, :].astype(BF16)

            @pl.when(needed >= row + ref.shape[0])
            def _(ref=ref):
                ref[...] = jnp.zeros_like(ref)


def attend(starts, q, do, keys, values, loads, stores, reach, first_head, count, carried=()):
    tok = q.shape[0]
    group = q.shape[1] // keys.shape[1]
    tq, tk = min(256, tok), min(128, tok)
    wide = group * tq
    seen = (reach + 1) * tok
    q_spec = pl.BlockSpec((tq, group * HEAD_SIZE), lambda g, i, s: (i, g + first_head))

    def kv_spec(rows, first):
        return pl.BlockSpec((rows, HEAD_SIZE), lambda g, i, s, first=first: (0, g + first))

    far_args, far_specs = [], []
    for array, k_block, v_block, _, _ in loads:
        far_args += [array, array]
        far_specs += [kv_spec(array.shape[0], k_block), kv_spec(array.shape[0], v_block)]
    part = pl.BlockSpec((tok, 2 * HEAD_SIZE), lambda g, i, s: (0, g))
    shape = (tok, 2 * count * HEAD_SIZE)
    before = 5 + len(far_args)
    results = pl.pallas_call(
        functools.partial(
            attend_body, tok, reach, group, tq, tk, [load[3:] for load in loads], stores, len(carried)
        ),
        grid_spec=pltpu.PrefetchScalarGridSpec(
            num_scalar_prefetch=1,
            grid=(count, tok // tq),
            in_specs=[q_spec, q_spec, kv_spec(tok, first_head), kv_spec(tok, first_head)]
            + far_specs
            + [pl.BlockSpec(memory_space=pl.ANY)] * len(carried),
            out_specs=[q_spec, q_spec] + [part] * (1 + len(stores)),
            scratch_shapes=[
                pltpu.VMEM((seen, HEAD_SIZE), BF16),
                pltpu.VMEM((seen, HEAD_SIZE), BF16),
                pltpu.VMEM((HEAD_SIZE, seen), BF16),
                pltpu.VMEM((HEAD_SIZE + SUM_ROWS, seen), BF16),
                pltpu.VMEM((seen, HEAD_SIZE), F32),
                pltpu.VMEM((seen, HEAD_SIZE), F32),
                pltpu.VMEM((seen, wide), F32),
                pltpu.VMEM((seen, wide), BF16),
                pltpu.VMEM((seen, wide), F32),
                pltpu.VMEM((HEAD_SIZE + SUM_ROWS, wide), F32),
                pltpu.VMEM((8, wide), F32),
            ],
        ),
        out_shape=[jax.ShapeDtypeStruct(q.shape, BF16)] * 2
        + [jax.ShapeDtypeStruct(shape, F32)]
        + [jax.ShapeDtypeStruct(shape, BF16)] * len(stores),
        input_output_aliases={before + n: n for n in range(len(carried))},
        compiler_params=pltpu.CompilerParams(vmem_limit_bytes=(12 << 20) + 10 * seen * wide),
        cost_estimate=pl.CostEstimate(
            flops=count * 5 * 10**9, bytes_accessed=count << 22, transcendentals=count * 4 * tok * tok
        ),
        name="attend",
    )(starts, q, do, keys, values, *far_args, *carried)
    return results[:2], results[2], results[3:]


def combine_body(counts, *refs):
    k_ref, v_ref = refs[-2:]
    at = 0
    for g, number in enumerate(counts):
        total = refs[at][...]
        for n in range(1, number):
            total = total + refs[at + n][...].astype(F32)
        at += number
        columns = slice(g * HEAD_SIZE, (g + 1) * HEAD_SIZE)
        k_ref[:, columns] = total[:, :HEAD_SIZE].astype(BF16)
        v_ref[:, columns] = total[:, HEAD_SIZE:].astype(BF16)


def combine(heads):
    tok = heads[0][0][0].shape[0]
    terms = [term for head in heads for term in head]
    specs = [pl.BlockSpec((tok, 2 * HEAD_SIZE), lambda i, block=block: (0, block)) for _, block in terms]
    shape = (tok, len(heads) * HEAD_SIZE)
    return pl.pallas_call(
        functools.partial(combine_body, [len(head) for head in heads]),
        grid=(1,),
        in_specs=specs,
        out_specs=[pl.BlockSpec(shape, lambda i: (0, 0))] * 2,
        out_shape=[jax.ShapeDtypeStruct(shape, BF16)] * 2,
        compiler_params=pltpu.CompilerParams(vmem_limit_bytes=COMBINE_VMEM),
        cost_estimate=pl.CostEstimate(flops=1 << 20, bytes_accessed=2 << 20, transcendentals=0),
        name="combine",
    )(*[array for array, _ in terms])


def always(rank):
    return rank >= 0


def any_length(tok, reach, starts, queries, keys, values, output_cotangent):
    kv_heads = keys.shape[1] // HEAD_SIZE
    packed = jnp.concatenate([keys, values], 1)
    loads = [
        (from_behind(packed, dist), 0, kv_heads, (reach - dist) * tok, always) for dist in range(1, reach + 1)
    ]
    stores = [(reach - dist) * tok for dist in range(1, reach + 1)]
    outs, own, parts = attend(
        starts, queries, output_cotangent, keys, values, loads, stores, reach, 0, kv_heads
    )
    back = [from_behind(part, -dist) for dist, part in enumerate(parts, 1)]
    return (*outs, *combine([[(x, g) for x in (own, *back)] for g in range(kv_heads)]))


def two_halves(tok, starts, queries, keys, values, output_cotangent):
    kv_heads = keys.shape[1] // HEAD_SIZE
    near = lax.ppermute(jnp.concatenate([keys, values], 1), "seq", [(0, 1), (2, 3)])
    across_keys = 2 * tok - starts[0]
    across_queries = starts[1] - 2 * tok
    crossing = (across_keys > 0) & (across_queries > 0)
    plan = jnp.where(crossing, jnp.where(across_keys > tok, 2, 1), 0)

    def apart(near):
        outs, own, parts = attend(
            starts, queries, output_cotangent, keys, values, [(near, 0, kv_heads, 0, always)], [0], 1, 0, kv_heads
        )
        back = lax.ppermute(parts[0], "seq", [(1, 0), (3, 2)])
        return (*outs, *combine([[(own, g), (back, g)] for g in range(kv_heads)]))

    def across(long, near):
        packed = []
        for g in range(kv_heads):
            own = [x[:, g * HEAD_SIZE : (g + 1) * HEAD_SIZE] for x in (keys, values)]
            block = jnp.concatenate(own, 1)
            if long:
                at = [x * HEAD_SIZE for x in (g, kv_heads + g)]
                behind = jnp.concatenate([near[:, x : x + HEAD_SIZE] for x in at], 1)
                block = jnp.concatenate([behind, block], 0)
            packed.append(block)
        first = [lax.ppermute(x, "seq", [(1, 2)]) for x in packed]
        if not long:
            second = [lax.ppermute(x, "seq", [(2, 3)]) for x in first]
        outs, terms, sent = (), [], ()
        for g in range(kv_heads):
            loads = [
                (near, g, kv_heads + g, tok, lambda rank: rank != 2),
                (first[g], 0, 1, 0 if long else tok, lambda rank: rank == 2),
            ]
            if not long:
                loads.append((second[g], 0, 1, 0, lambda rank: rank == 3))
            outs, own, parts = attend(
                starts, queries, output_cotangent, keys, values, loads, [tok, 0], 2, g, 1, outs
            )
            parts = lax.optimization_barrier((*parts, *sent))[:2]
            sent = (
                lax.ppermute(parts[0], "seq", [(1, 0), (2, 1), (3, 2)]),
                lax.ppermute(parts[1], "seq", [(2, 0)] if long else [(3, 1)]),
            )
            terms.append([(own, 0), (sent[0], 0), (sent[1], 0)])
        return (*outs, *combine(terms))

    return lax.switch(plan, [apart, functools.partial(across, False), functools.partial(across, True)], near)


def on_device(queries, keys, values, doc_ids, output_cotangent):
    tok = keys.shape[0]
    count = lax.axis_size("seq")
    numbers = lax.broadcasted_iota(jnp.int32, (DOCS - 1, 1), 0)
    before = jnp.sum((doc_ids[None, :] <= numbers).astype(jnp.int32), axis=1)
    starts = lax.psum(before, "seq")
    span = min(WINDOW, tok * count // 2)
    reach = min((span + tok - 2) // tok, count - 1)
    if count == 4 and span == 2 * tok and tok % 512 == 0:
        return tuple(two_halves(tok, starts, queries, keys, values, output_cotangent))
    return any_length(tok, reach, starts, queries, keys, values, output_cotangent)


def solution(mesh):
    wide = P(("grp", "seq"), "head")
    in_specs = (wide, wide, wide, P(("grp", "seq")), wide)
    return jax.shard_map(
        on_device, mesh=mesh, in_specs=in_specs, out_specs=(wide,) * 4, check_vma=False
    )
```

```python
import functools
import math

import jax
import jax.numpy as jnp
from jax import lax
from jax.experimental import pallas as pl
from jax.experimental.pallas import tpu as pltpu
from jax.sharding import PartitionSpec as P

HEAD_SIZE = 128
WINDOW = 2048
DOCS = 3

NEG_FILL = -1e30
F32 = jnp.float32
BF16 = jnp.bfloat16
SCALE = 1.0 / math.sqrt(HEAD_SIZE)
LOG2_SCALE = math.log2(math.e) / math.sqrt(HEAD_SIZE)
SUM_ROWS = 16
COMBINE_VMEM = 12 << 20


def from_behind(value, steps):
    count = lax.axis_size("seq")
    first, last = (max(0, -steps), min(count, count - steps))
    return lax.ppermute(value, "seq", [(source, source + steps) for source in range(first, last)])


def dot(a, b, ca=1, cb=0):
    return lax.dot_general(a, b, (((ca,), (cb,)), ((), ())), preferred_element_type=F32)


def fold_rows(value, op):
    total = value[0:8]
    for j in range(8, value.shape[0], 8):
        total = op(total, value[j : j + 8])
    return total


def attend_body(tok, reach, group, tq, tk, loads, stores, carried, starts, q_ref, do_ref, own_k, own_v, *rest):
    far_in, rest = rest[: 2 * len(loads)], rest[2 * len(loads) + carried :]
    o_ref, dq_ref, own_ref = rest[:3]
    far_out, rest = rest[3 : 3 + len(stores)], rest[3 + len(stores) :]
    k_all, v_all, kt_all, vt_all, dk_all, dv_all, s_buf, e_buf, dp_buf, acc, top = rest
    tile, tiles = pl.program_id(1), pl.num_programs(1)
    rank = lax.axis_index("seq")
    start_1, start_2, q_first = starts[0], starts[1], rank * tok
    k_base = q_first - reach * tok
    q_pos = q_first + tile * tq
    heads = range(group)

    def first_live(i):
        doc_start = jnp.where(i < start_1, 0, jnp.where(i < start_2, start_1, start_2))
        return jnp.maximum(doc_start, i - (WINDOW - 1))

    def load(first, k_ref, v_ref):
        k, v = k_ref[...], v_ref[...]
        rows = slice(first, first + k.shape[0])
        k_all[rows, :], v_all[rows, :] = k, v
        kt_all[:, rows], vt_all[:HEAD_SIZE, rows] = k.T, v.T
        vt_all[HEAD_SIZE:, rows] = jnp.ones((SUM_ROWS, k.shape[0]), BF16)
        dk_all[rows, :] = jnp.zeros(k.shape, F32)
        dv_all[rows, :] = jnp.zeros(v.shape, F32)

    @pl.when(tile == 0)
    def _():
        needed = first_live(q_first) - k_base
        load(reach * tok, own_k, own_v)
        for n, (first, when) in enumerate(loads):
            k_ref, v_ref = far_in[2 * n : 2 * n + 2]
            pl.when(when(rank) & (needed < first + k_ref.shape[0]))(functools.partial(load, first, k_ref, v_ref))

    low = jnp.maximum(first_live(q_pos) - k_base, 0) // tk
    units = (q_pos + tq - k_base) // tk - low
    last_first = first_live(q_pos + tq - 1)

    def over_keys(visit, most):
        def run(n, carry):
            visit(pl.multiple_of((low + most * n) * tk, tk), most * tk)
            return carry

        lax.fori_loop(0, units // most, run, 0)
        size = most // 2
        while size:

            @pl.when(units % (2 * size) >= size)
            def _(size=size):
                visit(pl.multiple_of((low + units // (2 * size) * (2 * size)) * tk, tk), size * tk)

            size //= 2

    q = jnp.concatenate([q_ref[:, h * HEAD_SIZE : (h + 1) * HEAD_SIZE] for h in heads], 0)
    do_t = jnp.concatenate([do_ref[:, h * HEAD_SIZE : (h + 1) * HEAD_SIZE].T for h in heads], 1)
    top[...] = jnp.full_like(top, NEG_FILL)

    def scores(off, size):
        s = dot(k_all[pl.ds(off, size), :], q, 1, 1)
        k_pos = k_base + off
        full = (k_pos >= last_first) & (k_pos + size - 1 <= q_pos)

        def put(s):
            s_buf[pl.ds(off, size), :] = s
            top[...] = jnp.maximum(top[...], fold_rows(s, jnp.maximum))

        @pl.when(full)
        def _():
            put(s)

        @pl.when(jnp.logical_not(full))
        def _():
            j = k_pos + lax.broadcasted_iota(jnp.int32, (size, tq), 0)
            i = q_pos + lax.broadcasted_iota(jnp.int32, (size, tq), 1)
            first = first_live(q_pos + lax.broadcasted_iota(jnp.int32, (1, tq), 1))
            live = (j <= i) & (j >= first)
            put(jnp.concatenate([jnp.where(live, s[:, h * tq : (h + 1) * tq], NEG_FILL) for h in heads], 1))

    over_keys(scores, 4)
    m = jnp.max(top[...], axis=0, keepdims=True)
    acc[...] = jnp.zeros_like(acc)

    def weigh(off, size):
        keys = pl.ds(off, size)
        dp_buf[keys, :] = dot(v_all[keys, :], do_t)
        eb = jnp.exp2((s_buf[keys, :] - m) * LOG2_SCALE).astype(BF16)
        e_buf[keys, :] = eb
        acc[...] += dot(vt_all[:, keys], eb)

    over_keys(weigh, 8 if reach == 1 else 4)
    inverse = 1.0 / acc[HEAD_SIZE : HEAD_SIZE + 1, :]
    out_t = (acc[:HEAD_SIZE, :] * inverse).astype(BF16)
    for h in heads:
        o_ref[:, h * HEAD_SIZE : (h + 1) * HEAD_SIZE] = out_t[:, h * tq : (h + 1) * tq].T
    delta = jnp.sum(do_t.astype(F32) * out_t.astype(F32), axis=0, keepdims=True) * inverse
    scaled_t = (do_t.astype(F32) * inverse).astype(BF16)
    scaled = jnp.concatenate([scaled_t[:, h * tq : (h + 1) * tq].T for h in heads], 0)
    acc[...] = jnp.zeros_like(acc)

    def back(off, size):
        keys = pl.ds(off, size)
        eb = e_buf[keys, :]
        dv_all[keys, :] += dot(eb, scaled)
        ds = (eb.astype(F32) * (dp_buf[keys, :] * inverse - delta)).astype(BF16)
        dk_all[keys, :] += dot(ds, q)
        acc[:HEAD_SIZE, :] += dot(kt_all[:, keys], ds)

    over_keys(back, 8 if reach == 1 else 4)
    dq_t = (acc[:HEAD_SIZE, :] * SCALE).astype(BF16)
    for h in heads:
        dq_ref[:, h * HEAD_SIZE : (h + 1) * HEAD_SIZE] = dq_t[:, h * tq : (h + 1) * tq].T

    @pl.when(tile == tiles - 1)
    def _():
        needed = first_live(q_first) - k_base
        own_ref[:, :HEAD_SIZE] = dk_all[reach * tok :, :] * SCALE
        own_ref[:, HEAD_SIZE:] = dv_all[reach * tok :, :]
        for ref, row in zip(far_out, stores):
            rows = slice(row, row + ref.shape[0])

            @pl.when(needed < row + ref.shape[0])
            def _(ref=ref, rows=rows):
                ref[:, :HEAD_SIZE] = (dk_all[rows, :] * SCALE).astype(BF16)
                ref[:, HEAD_SIZE:] = dv_all[rows, :].astype(BF16)

            @pl.when(needed >= row + ref.shape[0])
            def _(ref=ref):
                ref[...] = jnp.zeros_like(ref)


def attend(starts, q, do, keys, values, loads, stores, reach, first_head, count, carried=()):
    tok = q.shape[0]
    group = q.shape[1] // keys.shape[1]
    tq, tk = min(256, tok), min(128, tok)
    wide = group * tq
    seen = (reach + 1) * tok
    q_spec = pl.BlockSpec((tq, group * HEAD_SIZE), lambda g, i, s: (i, g + first_head))

    def kv_spec(rows, first):
        return pl.BlockSpec((rows, HEAD_SIZE), lambda g, i, s, first=first: (0, g + first))

    far_args, far_specs = [], []
    for array, k_block, v_block, _, _ in loads:
        far_args += [array, array]
        far_specs += [kv_spec(array.shape[0], k_block), kv_spec(array.shape[0], v_block)]
    part = pl.BlockSpec((tok, 2 * HEAD_SIZE), lambda g, i, s: (0, g))
    shape = (tok, 2 * count * HEAD_SIZE)
    before = 5 + len(far_args)
    results = pl.pallas_call(
        functools.partial(
            attend_body, tok, reach, group, tq, tk, [load[3:] for load in loads], stores, len(carried)
        ),
        grid_spec=pltpu.PrefetchScalarGridSpec(
            num_scalar_prefetch=1,
            grid=(count, tok // tq),
            in_specs=[q_spec, q_spec, kv_spec(tok, first_head), kv_spec(tok, first_head)]
            + far_specs
            + [pl.BlockSpec(memory_space=pl.ANY)] * len(carried),
            out_specs=[q_spec, q_spec] + [part] * (1 + len(stores)),
            scratch_shapes=[
                pltpu.VMEM((seen, HEAD_SIZE), BF16),
                pltpu.VMEM((seen, HEAD_SIZE), BF16),
                pltpu.VMEM((HEAD_SIZE, seen), BF16),
                pltpu.VMEM((HEAD_SIZE + SUM_ROWS, seen), BF16),
                pltpu.VMEM((seen, HEAD_SIZE), F32),
                pltpu.VMEM((seen, HEAD_SIZE), F32),
                pltpu.VMEM((seen, wide), F32),
                pltpu.VMEM((seen, wide), BF16),
                pltpu.VMEM((seen, wide), F32),
                pltpu.VMEM((HEAD_SIZE + SUM_ROWS, wide), F32),
                pltpu.VMEM((8, wide), F32),
            ],
        ),
        out_shape=[jax.ShapeDtypeStruct(q.shape, BF16)] * 2
        + [jax.ShapeDtypeStruct(shape, F32)]
        + [jax.ShapeDtypeStruct(shape, BF16)] * len(stores),
        input_output_aliases={before + n: n for n in range(len(carried))},
        compiler_params=pltpu.CompilerParams(vmem_limit_bytes=(20 << 20) + 10 * seen * wide),
        cost_estimate=pl.CostEstimate(
            flops=count * 5 * 10**9, bytes_accessed=count << 22, transcendentals=count * 4 * tok * tok
        ),
        name="attend",
    )(starts, q, do, keys, values, *far_args, *carried)
    return results[:2], results[2], results[3:]


def combine_body(counts, *refs):
    k_ref, v_ref = refs[-2:]
    at = 0
    for g, number in enumerate(counts):
        total = refs[at][...]
        for n in range(1, number):
            total = total + refs[at + n][...].astype(F32)
        at += number
        columns = slice(g * HEAD_SIZE, (g + 1) * HEAD_SIZE)
        k_ref[:, columns] = total[:, :HEAD_SIZE].astype(BF16)
        v_ref[:, columns] = total[:, HEAD_SIZE:].astype(BF16)


def combine(heads):
    tok = heads[0][0][0].shape[0]
    terms = [term for head in heads for term in head]
    specs = [pl.BlockSpec((tok, 2 * HEAD_SIZE), lambda i, block=block: (0, block)) for _, block in terms]
    shape = (tok, len(heads) * HEAD_SIZE)
    return pl.pallas_call(
        functools.partial(combine_body, [len(head) for head in heads]),
        grid=(1,),
        in_specs=specs,
        out_specs=[pl.BlockSpec(shape, lambda i: (0, 0))] * 2,
        out_shape=[jax.ShapeDtypeStruct(shape, BF16)] * 2,
        compiler_params=pltpu.CompilerParams(vmem_limit_bytes=COMBINE_VMEM),
        cost_estimate=pl.CostEstimate(flops=1 << 20, bytes_accessed=2 << 20, transcendentals=0),
        name="combine",
    )(*[array for array, _ in terms])


def always(rank):
    return rank >= 0


def any_length(tok, reach, starts, queries, keys, values, output_cotangent):
    kv_heads = keys.shape[1] // HEAD_SIZE
    packed = jnp.concatenate([keys, values], 1)
    loads = [
        (from_behind(packed, dist), 0, kv_heads, (reach - dist) * tok, always) for dist in range(1, reach + 1)
    ]
    stores = [(reach - dist) * tok for dist in range(1, reach + 1)]
    outs, own, parts = attend(
        starts, queries, output_cotangent, keys, values, loads, stores, reach, 0, kv_heads
    )
    back = [from_behind(part, -dist) for dist, part in enumerate(parts, 1)]
    return (*outs, *combine([[(x, g) for x in (own, *back)] for g in range(kv_heads)]))


def two_halves(tok, starts, queries, keys, values, output_cotangent):
    kv_heads = keys.shape[1] // HEAD_SIZE
    near = lax.ppermute(jnp.concatenate([keys, values], 1), "seq", [(0, 1), (2, 3)])
    across_keys = 2 * tok - starts[0]
    across_queries = starts[1] - 2 * tok
    crossing = (across_keys > 0) & (across_queries > 0)
    plan = jnp.where(crossing, jnp.where(across_keys > tok, 2, 1), 0)

    def apart(near):
        outs, own, parts = attend(
            starts, queries, output_cotangent, keys, values, [(near, 0, kv_heads, 0, always)], [0], 1, 0, kv_heads
        )
        back = lax.ppermute(parts[0], "seq", [(1, 0), (3, 2)])
        return (*outs, *combine([[(own, g), (back, g)] for g in range(kv_heads)]))

    def across(long, near):
        packed = []
        for g in range(kv_heads):
            own = [x[:, g * HEAD_SIZE : (g + 1) * HEAD_SIZE] for x in (keys, values)]
            block = jnp.concatenate(own, 1)
            if long:
                at = [x * HEAD_SIZE for x in (g, kv_heads + g)]
                behind = jnp.concatenate([near[:, x : x + HEAD_SIZE] for x in at], 1)
                block = jnp.concatenate([behind, block], 0)
            packed.append(block)
        first = [lax.ppermute(x, "seq", [(1, 2)]) for x in packed]
        if not long:
            second = [lax.ppermute(x, "seq", [(2, 3)]) for x in first]
        outs, terms, sent = (), [], ()
        for g in range(kv_heads):
            loads = [
                (near, g, kv_heads + g, tok, lambda rank: rank != 2),
                (first[g], 0, 1, 0 if long else tok, lambda rank: rank == 2),
            ]
            if not long:
                loads.append((second[g], 0, 1, 0, lambda rank: rank == 3))
            outs, own, parts = attend(
                starts, queries, output_cotangent, keys, values, loads, [tok, 0], 2, g, 1, outs
            )
            parts = lax.optimization_barrier((*parts, *sent))[:2]
            sent = (
                lax.ppermute(parts[0], "seq", [(1, 0), (2, 1), (3, 2)]),
                lax.ppermute(parts[1], "seq", [(2, 0)] if long else [(3, 1)]),
            )
            terms.append([(own, 0), (sent[0], 0), (sent[1], 0)])
        return (*outs, *combine(terms))

    return lax.switch(plan, [apart, functools.partial(across, False), functools.partial(across, True)], near)


def on_device(queries, keys, values, doc_ids, output_cotangent):
    tok = keys.shape[0]
    count = lax.axis_size("seq")
    numbers = lax.broadcasted_iota(jnp.int32, (DOCS - 1, 1), 0)
    before = jnp.sum((doc_ids[None, :] <= numbers).astype(jnp.int32), axis=1)
    starts = lax.psum(before, "seq")
    span = min(WINDOW, tok * count // 2)
    reach = min((span + tok - 2) // tok, count - 1)
    if count == 4 and span == 2 * tok and tok % 512 == 0:
        return tuple(two_halves(tok, starts, queries, keys, values, output_cotangent))
    return any_length(tok, reach, starts, queries, keys, values, output_cotangent)


def solution(mesh):
    wide = P(("grp", "seq"), "head")
    in_specs = (wide, wide, wide, P(("grp", "seq")), wide)
    return jax.shard_map(
        on_device, mesh=mesh, in_specs=in_specs, out_specs=(wide,) * 4, check_vma=False
    )
```
